32 devices in a mesh: tile: 16 (over z, y, core), slide: 2 (over x).
Axes of the slice: x: 2, y: 2, z: 4, core: 2. Of those that a mesh axis runs over, the one named last changes fastest.
Arguments:
- feats: bfloat16 [2, 64, 1024, 128], P('slide', 'tile'), may hold values from -6 to 6
- cotangent: bfloat16 [2, 64, 1024, 128], P('slide', 'tile'), may hold values from -6 to 6
- w_reduce: bfloat16 [512, 1024], replicated, may hold values from -0.1875 to 0.1875
- w_group: bfloat16 [512, 144], replicated, may hold values from -0.5 to 0.5
- w_expand: bfloat16 [512, 1024], replicated, may hold values from -0.25 to 0.25
- scale1: float32 [512], replicated, may hold values from 0.25 to 1.75
- shift1: float32 [512], replicated, may hold values from -3 to 3
- scale2: float32 [512], replicated, may hold values from 0.25 to 1.75
- shift2: float32 [512], replicated, may hold values from -3 to 3
- scale3: float32 [1024], replicated, may hold values from 0.25 to 1.75
- shift3: float32 [1024], replicated, may hold values from -3 to 3
- tile_count: int32 [2, 16], P('slide'), may hold values from 1 to 4, as said below
- joined: int32 [2, 31], P('slide'), may hold values 0 or 1
Outputs:
- out: bfloat16 [2, 64, 1024, 128], P('slide', 'tile')
- grad_feats: bfloat16 [2, 64, 1024, 128], P('slide', 'tile')
- grad_reduce: float32 [512, 1024], P('tile')
- grad_group: float32 [512, 144], P('tile')
- grad_expand: float32 [512, 1024], P('tile')
The draws below stay inside these ranges and needn't reach their ends.
Inputs may be any that keep to these rules, and one draw needn't show every extreme that they name: `tile_count`: each device of a slide holds 1 to 4 tissue tiles, and some device of every slide holds exactly 4; a slide holds 32 tissue tiles in all; the tiles held by devices 0 .. d-1 of a slide number 2d-1, 2d or 2d+1.
All inputs are finite; a program needn't handle non-finite values. No bound on the sum of `joined` on one device may be relied on, other than what follows from the above.
Results may differ from the reference program's by a relative error of at most 0.0064.
Values may be sent and summed in bfloat16 or wider, within the bound.
No kernel may reach another device: no remote copies, remote signals or barrier semaphores. Data moves between devices by JAX's collectives and lax.ppermute only.
A program may use at most 128 MiB of HBM per device.

```python
import math
import jax
import jax.numpy as jnp
import numpy as np
from jax import lax

CIN = 1024
MID = 512
GROUPS = 32
GW = 16
TH = 16
TW = 8
PIX = 128
SLOTS = 4
TILES = 64
LIVE = 32
SLIDES = 2


count_patterns = np.array([[1, 4, 1, 2], [1, 4, 2, 1], [1, 2, 4, 1], [2, 1, 4, 1], [2, 2, 2, 2], [1, 3, 2, 2], [2, 1, 3, 2], [3, 1, 2, 2], [2, 2, 1, 3], [1, 3, 1, 3], [3, 2, 1, 2], [3, 1, 3, 1]], dtype=np.int32)


def draw_tile_count(key, part):
    blocks = TILES // SLOTS // 4
    pattern_table = jnp.asarray(count_patterns)
    pattern_picks = jax.random.randint(jax.random.fold_in(key, 11), (SLIDES, blocks), 0, 12)
    forced_block = jax.random.randint(jax.random.fold_in(key, 12), (SLIDES, 1), 0, blocks)
    forced_kind = jax.random.randint(jax.random.fold_in(key, 13), (SLIDES, 1), 0, 4)
    columns = jnp.arange(blocks, dtype=jnp.int32)[None, :]
    chosen = jnp.where(columns == forced_block, forced_kind, pattern_picks)
    return jnp.take(pattern_table, chosen, axis=0).reshape(SLIDES, blocks * 4).astype(jnp.int32)


def place_ends(drawn, own_key, low, top_value):
    dims = drawn.shape
    place = [jax.random.randint(jax.random.fold_in(own_key, axis), (), 0, dims[axis]) for axis in range(len(dims))]
    drawn = drawn.at[tuple(place)].set(low)
    longest = dims.index(max(dims))
    place[longest] = (place[longest] + 1) % dims[longest]
    return drawn.at[tuple(place)].set(top_value)


def block_levels(stream_key, extent, split, least, top_value):
    gain, own = 1.0, jax.random.fold_in(stream_key, 6)
    for dim, shards_of in split:
        draws = jnp.exp(jax.random.uniform(jax.random.fold_in(own, dim), (shards_of,), jnp.float32, least / len(split), top_value / len(split)))
        gain = gain * jnp.repeat(draws, extent[dim] // shards_of).reshape([-1 if axis == dim else 1 for axis in range(len(extent))])
    return gain


def scatter_about(stream_key, dims, spread, most, cuts=(), kind=jnp.bfloat16):
    level = block_levels(stream_key, dims, cuts, -0.22, 0.18) if cuts else 1.0
    drawn = jax.random.normal(stream_key, dims, jnp.float32) * spread * level
    return jnp.minimum(jnp.maximum(drawn, -most), most).astype(kind)


def setup_inputs(seed: int = 0) -> dict:
    keys = jax.random.split(jax.random.key(seed), 14)
    feats = scatter_about(keys[0], (SLIDES, TILES, CIN, PIX), 1.0, 6.0, ((0, 2), (1, 16)))
    cotangent = scatter_about(keys[1], (SLIDES, TILES, CIN, PIX), 1.0, 6.0, ((0, 2), (1, 16)))
    w_reduce = scatter_about(keys[2], (MID, CIN), CIN ** -0.5, 0.1875)
    w_group = scatter_about(keys[3], (MID, 9 * GW), (9 * GW) ** -0.5, 0.5)
    w_expand = scatter_about(keys[4], (MID, CIN), MID ** -0.5, 0.25)
    scale1 = jnp.clip(1.0 + 0.15 * jax.random.normal(keys[5], (MID,), jnp.float32), 0.25, 1.75)
    shift1 = scatter_about(keys[6], (MID,), 0.5, 3.0, (), jnp.float32)
    scale2 = jnp.clip(1.0 + 0.15 * jax.random.normal(keys[7], (MID,), jnp.float32), 0.25, 1.75)
    shift2 = scatter_about(keys[8], (MID,), 0.5, 3.0, (), jnp.float32)
    scale3 = jnp.clip(1.0 + 0.15 * jax.random.normal(keys[9], (CIN,), jnp.float32), 0.25, 1.75)
    shift3 = scatter_about(keys[10], (CIN,), 0.5, 3.0, (), jnp.float32)
    tile_count = draw_tile_count(jax.random.fold_in(keys[13], 71), 0)
    joined = place_ends((jax.random.randint(keys[12], (SLIDES, LIVE - 1), 0, 4) < 3).astype(jnp.int32), jax.random.fold_in(keys[12], 1), 0, 1)
    return {"feats": feats, "cotangent": cotangent, "w_reduce": w_reduce, "w_group": w_group, "w_expand": w_expand, "scale1": scale1, "shift1": shift1, "scale2": scale2, "shift2": shift2, "scale3": scale3, "shift3": shift3, "tile_count": tile_count, "joined": joined}


def activate(values):
    return values * jax.nn.sigmoid(values)

def slope(values):
    sigmoid_v = jax.nn.sigmoid(values)
    return sigmoid_v + values * sigmoid_v * (1.0 - sigmoid_v)

def band_slots(slide_counts):
    starts = (jnp.cumsum(slide_counts) - slide_counts).astype(jnp.int32)
    band_index = jnp.arange(LIVE, dtype=jnp.int32)
    owner = lax.optimization_barrier(jnp.sum((starts[1:][None, :] <= band_index[:, None]).astype(jnp.int32), axis=1)).astype(jnp.int32)
    within = (band_index - jnp.take(starts, owner)).astype(jnp.int32)
    return (owner * SLOTS + within).astype(jnp.int32)

def frame_up(field_map, seam_links):
    tile_total, channels = (field_map.shape[0], field_map.shape[1])
    grid_view = field_map.reshape(tile_total, channels, TH, TW)
    zero_col = jnp.zeros_like(grid_view[:1, :, :, 0])
    before_col = jnp.concatenate([zero_col, grid_view[:-1, :, :, -1]], 0)
    after_col = jnp.concatenate([grid_view[1:, :, :, 0], zero_col], 0)
    link_values = seam_links.astype(field_map.dtype)
    zero_link = jnp.zeros((1,), field_map.dtype)
    before_col = before_col * jnp.concatenate([zero_link, link_values])[:, None, None]
    after_col = after_col * jnp.concatenate([link_values, zero_link])[:, None, None]
    widened = jnp.concatenate([before_col[..., None], grid_view, after_col[..., None]], 3)
    return jnp.pad(widened, ((0, 0), (0, 0), (1, 1), (0, 0)))

def group_apply(framed_map, kernel, transposed):
    tile_total = framed_map.shape[0]
    tap_weights = kernel.astype(jnp.float32).reshape(GROUPS, GW, 9, GW)
    summed = jnp.zeros((tile_total, GROUPS, GW, TH * TW), jnp.float32)
    for offset in range(9):
        row_off, col_off = (offset // 3, offset % 3)
        if transposed:
            window = framed_map[:, :, 2 - row_off:2 - row_off + TH, 2 - col_off:2 - col_off + TW]
            window = window.astype(jnp.float32).reshape(tile_total, GROUPS, GW, TH * TW)
            summed = summed + jnp.einsum('goi,ngop->ngip', tap_weights[:, :, offset, :], window)
        else:
            window = framed_map[:, :, row_off:row_off + TH, col_off:col_off + TW]
            window = window.astype(jnp.float32).reshape(tile_total, GROUPS, GW, TH * TW)
            summed = summed + jnp.einsum('goi,ngip->ngop', tap_weights[:, :, offset, :], window)
    return summed.reshape(tile_total, GROUPS * GW, TH * TW)

def group_weight_grad(errors, framed_map):
    tile_total = framed_map.shape[0]
    grouped_err = errors.astype(jnp.float32).reshape(tile_total, GROUPS, GW, TH * TW)
    tap_grads = []
    for offset in range(9):
        row_off, col_off = (offset // 3, offset % 3)
        window = framed_map[:, :, row_off:row_off + TH, col_off:col_off + TW]
        window = window.astype(jnp.float32).reshape(tile_total, GROUPS, GW, TH * TW)
        tap_grads.append(jnp.einsum('ngop,ngip->goi', grouped_err, window))
    return jnp.stack(tap_grads, 2).reshape(GROUPS * GW, 9 * GW)

def reference(feats, cotangent, w_reduce, w_group, w_expand, scale1, shift1, scale2, shift2, scale3, shift3, tile_count, joined):
    reduce_f = w_reduce.astype(jnp.float32)
    expand_f = w_expand.astype(jnp.float32)

    def one_slide(inputs):
        slide_feats, slide_cot, slide_counts, seam_links = inputs
        slot_index = band_slots(slide_counts)
        tiles_in = jnp.take(slide_feats, slot_index, axis=0)
        cot_in = jnp.take(slide_cot, slot_index, axis=0)
        tiles_f = tiles_in.astype(jnp.float32)
        pre_reduce = jnp.einsum('oc,ncp->nop', reduce_f, tiles_f) * scale1[:, None] + shift1[:, None]
        hidden_a = activate(pre_reduce).astype(jnp.bfloat16)
        frame_a = frame_up(hidden_a, seam_links)
        pre_group = group_apply(frame_a, w_group, False) * scale2[:, None] + shift2[:, None]
        hidden_b = activate(pre_group).astype(jnp.bfloat16)
        residual_sum = jnp.einsum('oc,nop->ncp', expand_f, hidden_b.astype(jnp.float32)) * scale3[:, None] + shift3[:, None] + tiles_f
        outputs = activate(residual_sum).astype(jnp.bfloat16)
        back_grad = cot_in.astype(jnp.float32) * slope(residual_sum)
        error_c = (back_grad * scale3[:, None]).astype(jnp.bfloat16)
        error_b = (jnp.einsum('oc,ncp->nop', expand_f, error_c.astype(jnp.float32)) * slope(pre_group) * scale2[:, None]).astype(jnp.bfloat16)
        frame_b = frame_up(error_b, seam_links)
        error_a = (group_apply(frame_b, w_group, True) * slope(pre_reduce) * scale1[:, None]).astype(jnp.bfloat16)
        grad_in = (jnp.einsum('oc,nop->ncp', reduce_f, error_a.astype(jnp.float32)) + back_grad).astype(jnp.bfloat16)
        part_reduce = jnp.einsum('nop,ncp->oc', error_a.astype(jnp.float32), tiles_f)
        part_group = group_weight_grad(error_b, frame_a)
        part_expand = jnp.einsum('nop,ncp->oc', hidden_b.astype(jnp.float32), error_c.astype(jnp.float32))
        out_home = jnp.zeros((TILES, CIN, TH * TW), jnp.bfloat16).at[slot_index].set(outputs)
        grad_home = jnp.zeros((TILES, CIN, TH * TW), jnp.bfloat16).at[slot_index].set(grad_in)
        return (out_home, grad_home, part_reduce, part_group, part_expand)
    results = lax.map(one_slide, (feats, cotangent, tile_count, joined))
    norm = 1.0 / math.sqrt(SLIDES * LIVE * TH * TW)
    grad_reduce = lax.optimization_barrier(jnp.sum(results[2], 0)) * norm
    grad_group = lax.optimization_barrier(jnp.sum(results[3], 0)) * norm
    grad_expand = lax.optimization_barrier(jnp.sum(results[4], 0)) * norm
    return (results[0], results[1], grad_reduce, grad_group, grad_expand)
```

```python
import functools
import math

import jax
import jax.numpy as jnp
from jax import lax
from jax.experimental import pallas as pl
from jax.experimental.pallas import tpu as pltpu
from jax.sharding import PartitionSpec as P

CIN = 1024
MID = 512
GW = 16
TH = 16
TW = 8
PIX = 128
SLOTS = 4
HALF = 256
TAPS = 9
KDIM = TAPS * HALF
PAY = 48
LIVE_DEV = 2
BF = jnp.bfloat16
F32 = jnp.float32
VMEM_LIMIT = 56 * 1024 * 1024

HELD, L_LINK, R_LINK, L_IDX, R_IDX, META = 0, 1, 6, 11, 16, 24


def nt_dot(a, b):
    return lax.dot_general(a, b, (((1,), (1,)), ((), ())), preferred_element_type=F32)


def tn_dot(a, b):
    return lax.dot_general(a, b, (((0,), (0,)), ((), ())), preferred_element_type=F32)


def nn_dot(a, b):
    return lax.dot_general(a, b, (((1,), (0,)), ((), ())), preferred_element_type=F32)


def sigmoid(v):
    return 0.5 * jnp.tanh(0.5 * v) + 0.5


def column(row_ref):
    row = row_ref[...]
    return jnp.transpose(jnp.broadcast_to(row, (PIX, row.shape[1])))


def wide(col, lanes):
    return jnp.concatenate([col] * (lanes // PIX), axis=1)


def edge_select(rows, lane_of):
    row = lax.broadcasted_iota(jnp.int32, (rows, PIX), 0)
    lane = lax.broadcasted_iota(jnp.int32, (rows, PIX), 1)
    return (lane == lane_of(row)).astype(F32).astype(BF)


def x_lane(first):
    return lambda row: (row % TH) * TW + row // TH + first


def g_lane(col):
    return lambda row: row * TW + col


def edge_kernel(count_ref, joined_ref, x_any, g_any, core_ref, other_ref, meta_ref, xbuf, gbuf, sems):
    me = lax.axis_index("tile")
    devices = count_ref.shape[1]
    links = joined_ref.shape[1]
    start = jnp.int32(0)
    held = jnp.int32(0)
    for e in range(devices):
        start = start + jnp.where(e < me, count_ref[0, e], 0)
        held = held + jnp.where(e == me, count_ref[0, e], 0)
    last = held - 1
    copies = []
    for k, (src, dst, slot) in enumerate(
        ((x_any, xbuf, 0), (g_any, gbuf, 0), (x_any, xbuf, last), (g_any, gbuf, last))
    ):
        copy = pltpu.make_async_copy(src.at[slot], dst.at[k // 2], sems.at[k])
        copy.start()
        copies.append(copy)

    def link(at):
        inside = jnp.logical_and(at >= 0, at < links)
        return jnp.where(inside, joined_ref[0, jnp.clip(at, 0, links - 1)], 0)

    meta_ref[HELD] = held
    first_left = link(start - 1)
    last_right = link(start + last)
    for i in range(SLOTS):
        live = i < held
        meta_ref[L_LINK + i] = jnp.where(live, link(start + i - 1), 0)
        meta_ref[R_LINK + i] = jnp.where(live, link(start + i), 0)
        meta_ref[L_IDX + i] = jnp.int32(SLOTS if i == 0 else i - 1)
        meta_ref[R_IDX + i] = jnp.where(i >= last, SLOTS, i + 1).astype(jnp.int32)
    meta_ref[L_LINK + SLOTS] = last_right
    meta_ref[R_LINK + SLOTS] = first_left
    meta_ref[L_IDX + SLOTS] = last
    meta_ref[R_IDX + SLOTS] = jnp.int32(0)

    for copy in copies:
        copy.wait()
    even = me % 2 == 0

    def payload(side, x_first, g_col):
        return (
            nt_dot(edge_select(2 * TH, x_lane(x_first)), xbuf[side]).astype(BF),
            nt_dot(edge_select(TH, g_lane(g_col)), gbuf[side]).astype(BF),
        )

    left_x, left_g = payload(0, 0, 0)
    right_x, right_g = payload(1, TW - 2, TW - 1)

    @pl.when(even)
    def _():
        core_ref[: 2 * TH] = right_x
        core_ref[2 * TH :] = right_g
        other_ref[: 2 * TH] = left_x
        other_ref[2 * TH :] = left_g

    @pl.when(jnp.logical_not(even))
    def _():
        core_ref[: 2 * TH] = left_x
        core_ref[2 * TH :] = left_g
        other_ref[: 2 * TH] = right_x
        other_ref[2 * TH :] = right_g


def prep_kernel(
    meta_ref, x_ref, wr_ref, we_ref, wg_ref, s1_ref, b1_ref,
    hid_ref, slope_ref, dense_ref, denset_ref, wet_ref,
):
    scale = column(s1_ref)
    shift = column(b1_ref)
    held = meta_ref[HELD]
    for half in range(SLOTS // 2):
        tiles = jnp.concatenate([x_ref[2 * half], x_ref[2 * half + 1]], axis=1)
        reduced = nn_dot(wr_ref[...], tiles)
        for k in range(2):
            i = 2 * half + k
            pre = reduced[:, k * PIX : (k + 1) * PIX] * scale + shift
            sig = sigmoid(pre)
            act = pre * sig
            hid_ref[i] = act.astype(BF)
            live = jnp.where(i < held, 1.0, 0.0).astype(F32)
            slope_ref[i] = (sig + act * (1.0 - sig)) * (scale * live)
    tap_row = lax.broadcasted_iota(jnp.int32, (TAPS * GW, KDIM), 0)
    lane = lax.broadcasted_iota(jnp.int32, (TAPS * GW, KDIM), 1)
    pick = (tap_row == (lane // HALF) * GW + lane % GW).astype(F32).astype(BF)
    spread = nn_dot(wg_ref[...], pick)
    row = lax.broadcasted_iota(jnp.int32, (MID, KDIM), 0)
    col = lax.broadcasted_iota(jnp.int32, (MID, KDIM), 1)
    keep = (row % HALF) // GW == (col % HALF) // GW
    dense_ref[...] = jnp.where(keep, spread, 0.0).astype(BF).reshape(2, HALF, KDIM)
    row_t = lax.broadcasted_iota(jnp.int32, (HALF, MID), 0)
    col_t = lax.broadcasted_iota(jnp.int32, (HALF, MID), 1)
    keep_t = row_t // GW == (col_t % HALF) // GW
    prow = lax.broadcasted_iota(jnp.int32, (HALF, TAPS * GW), 0)
    pcol = lax.broadcasted_iota(jnp.int32, (HALF, TAPS * GW), 1)
    for k in range(TAPS):
        pick_t = (pcol == k * GW + prow % GW).astype(F32).astype(BF)
        spread_t = jnp.where(keep_t, nt_dot(pick_t, wg_ref[...]), 0.0).astype(BF)
        for b in range(2):
            denset_ref[b, :, k * HALF : (k + 1) * HALF] = spread_t[:, b * HALF : (b + 1) * HALF]
    wet_ref[...] = jnp.transpose(we_ref[...])


def build_windows(field_ref, win_ref, meta_ref, tiles, transposed):
    lane = lax.broadcasted_iota(jnp.int32, (HALF, PIX), 1)
    col = lane % TW
    first_col = col == 0
    last_col = col == TW - 1
    has_above = lane >= TW
    has_below = lane < PIX - TW
    for i in range(tiles):
        left_at = meta_ref[L_IDX + i]
        right_at = meta_ref[R_IDX + i]
        left_link = meta_ref[L_LINK + i].astype(F32)
        right_link = meta_ref[R_LINK + i].astype(F32)
        lanes = pl.ds(i * PIX, PIX)
        for b in range(2):
            rows = pl.ds(b * HALF, HALF)
            own = field_ref[i, rows, :].astype(F32)
            left = field_ref[left_at, rows, :].astype(F32) * left_link
            right = field_ref[right_at, rows, :].astype(F32) * right_link
            west = jnp.where(first_col, pltpu.roll(left, PIX - TW + 1, 1), pltpu.roll(own, 1, 1))
            east = jnp.where(last_col, pltpu.roll(right, TW - 1, 1), pltpu.roll(own, PIX - 1, 1))
            for v, base in enumerate((west, own, east)):
                above = jnp.where(has_above, pltpu.roll(base, TW, 1), 0.0)
                below = jnp.where(has_below, pltpu.roll(base, PIX - TW, 1), 0.0)
                for u, shifted in enumerate((above, base, below)):
                    tap = 3 * u + v
                    if transposed:
                        tap = TAPS - 1 - tap
                    win_ref[b, pl.ds(tap * HALF, HALF), lanes] = shifted.astype(BF)


def forward_kernel(
    devices, meta_ref, core_ref, other_ref, hid_in, wr_ref, s1_ref, b1_ref, dense_ref,
    s2_ref, b2_ref, wet_ref, we_ref, s3_ref, b3_ref, x_ref, g_ref,
    out_ref, back_ref, errb_ref, send_ref, keep_ref,
    hid_ref, win_ref, hidb_ref, slopeb_ref, errc_ref,
):
    me = lax.axis_index("tile")
    held = meta_ref[HELD]
    odd = me % 2
    scale1 = column(s1_ref)
    shift1 = column(b1_ref)
    core_first = jnp.where(odd == 0, 0, TW - 2)
    other_first = jnp.where(odd == 0, TW - 2, 0)
    core_g = jnp.where(odd == 0, 0, TW - 1)
    other_g = jnp.where(odd == 0, TW - 1, 0)
    edge_x = (
        tn_dot(core_ref[: 2 * TH, :], edge_select(2 * TH, x_lane(core_first)))
        + tn_dot(other_ref[: 2 * TH, :], edge_select(2 * TH, x_lane(other_first)))
    ).astype(BF)
    edge_g = (
        tn_dot(core_ref[2 * TH :, :], edge_select(TH, g_lane(core_g)))
        + tn_dot(other_ref[2 * TH :, :], edge_select(TH, g_lane(other_g)))
    )
    for i in range(SLOTS):
        hid_ref[i] = hid_in[i]
    pre = nn_dot(wr_ref[...], edge_x) * scale1 + shift1
    hid_ref[SLOTS] = (pre * sigmoid(pre)).astype(BF)

    build_windows(hid_ref, win_ref, meta_ref, SLOTS + 1, False)

    scale2 = column(s2_ref)
    shift2 = column(b2_ref)
    for b in range(2):
        conv = nn_dot(dense_ref[b], win_ref[b])
        rows = slice(b * HALF, (b + 1) * HALF)
        for i in range(SLOTS + 1):
            v = conv[:, i * PIX : (i + 1) * PIX] * scale2[rows] + shift2[rows]
            sig = sigmoid(v)
            act = v * sig
            hidb_ref[rows, i * PIX : (i + 1) * PIX] = act.astype(BF)
            slopeb_ref[rows, i * PIX : (i + 1) * PIX] = (sig + act * (1.0 - sig)) * scale2[rows]

    scale3 = column(s3_ref)
    shift3 = column(b3_ref)
    for first, count in ((0, 2), (2, 2), (4, 1)):
        grown = nn_dot(wet_ref[...], hidb_ref[:, first * PIX : (first + count) * PIX])
        for k in range(count):
            i = first + k
            if i < SLOTS:
                tile = x_ref[i].astype(F32)
                cot = g_ref[i].astype(F32)
            else:
                tile = edge_x.astype(F32)
                cot = edge_g
            total = grown[:, k * PIX : (k + 1) * PIX] * scale3 + shift3 + tile
            sig = sigmoid(total)
            act = total * sig
            back = cot * (sig + act * (1.0 - sig))
            if i < SLOTS:
                live = jnp.where(i < held, 1.0, 0.0).astype(F32)
                back = back * live
                out_ref[i] = (act * live).astype(BF)
                back_ref[i] = back
            errc_ref[:, i * PIX : (i + 1) * PIX] = (back * scale3).astype(BF)

    order_rows(devices, me, hidb_ref, errc_ref, SLOTS * PIX, send_ref, keep_ref)

    for first, count in ((0, 2), (2, 2), (4, 1)):
        lanes = slice(first * PIX, (first + count) * PIX)
        pulled = nn_dot(we_ref[...], errc_ref[:, lanes])
        errb = (pulled * slopeb_ref[:, lanes]).astype(BF)
        for k in range(count):
            errb_ref[first + k] = errb[:, k * PIX : (k + 1) * PIX]


def order_rows(devices, me, left_ref, right_ref, lanes, send_ref, keep_ref):
    per = MID // devices
    for ref, flip in ((send_ref, 1), (keep_ref, 0)):
        picked = []
        for pair in range(devices // 2):
            dy, rest = pair // (devices // 4), pair % (devices // 4)
            target = (rest * 4) + (((me // 2) % 2) ^ dy) * 2 + ((me % 2) ^ flip)
            at = pl.multiple_of(target * per, per)
            picked.append(left_ref[pl.ds(at, per), :lanes])
        rows = jnp.concatenate(picked, axis=0)
        ref[...] = nt_dot(rows, right_ref[:, :lanes]).astype(BF)


def backward_kernel(
    devices, meta_ref, errb_ref, hid_ref, slope_ref, denset_ref, x_ref,
    erra_ref, send_ref, keep_ref, win_ref, flat_ref, groups_ref,
):
    me = lax.axis_index("tile")
    build_windows(errb_ref, win_ref, meta_ref, SLOTS, True)
    for b in range(2):
        conv = nn_dot(denset_ref[b], win_ref[b])
        rows = slice(b * HALF, (b + 1) * HALF)
        for i in range(SLOTS):
            err = (conv[:, i * PIX : (i + 1) * PIX] * slope_ref[i, rows, :]).astype(BF)
            flat_ref[rows, i * PIX : (i + 1) * PIX] = err
            erra_ref[i, rows, :] = err
    row = lax.broadcasted_iota(jnp.int32, (HALF, HALF), 0)
    col = lax.broadcasted_iota(jnp.int32, (HALF, HALF), 1)
    same = row // GW == col // GW
    for b in range(2):
        rows = slice(b * HALF, (b + 1) * HALF)
        hid = jnp.concatenate([hid_ref[i, rows, :] for i in range(SLOTS)], axis=1)
        folded = jnp.zeros((HALF, HALF), F32)
        for k in range(TAPS):
            full = nt_dot(win_ref[b, k * HALF : (k + 1) * HALF, :], hid)
            kept = jnp.where(same, full, 0.0).astype(BF)
            place = (col == k * GW + row % GW).astype(F32).astype(BF)
            folded = folded + nn_dot(kept, place)
        groups_ref[rows, :] = folded.astype(BF)
    tiles = jnp.concatenate([x_ref[i] for i in range(SLOTS)], axis=1)
    per = MID // devices
    for ref, flip in ((send_ref, 1), (keep_ref, 0)):
        picked, group_rows = [], []
        for pair in range(devices // 2):
            target = pair * 2 + ((me % 2) ^ flip)
            at = pl.multiple_of(target * per, per)
            picked.append(flat_ref[pl.ds(at, per), :])
            ref[pl.ds(pair * per, per), CIN:] = groups_ref[pl.ds(at, per), :]
        rows = jnp.concatenate(picked, axis=0)
        ref[:, :CIN] = nt_dot(rows, tiles).astype(BF)


def grad_kernel(wr_ref, erra_ref, back_ref, grad_ref):
    for half in range(SLOTS // 2):
        err = jnp.concatenate([erra_ref[2 * half], erra_ref[2 * half + 1]], axis=1)
        pulled = tn_dot(wr_ref[...], err)
        for k in range(2):
            i = 2 * half + k
            grad_ref[i] = (pulled[:, k * PIX : (k + 1) * PIX] + back_ref[i]).astype(BF)


def call(body, name, out_shape, in_smem, in_any, n_in, scratch=(), out_smem=()):
    vmem = pl.BlockSpec(memory_space=pltpu.VMEM)
    smem = pl.BlockSpec(memory_space=pltpu.SMEM)
    anys = pl.BlockSpec(memory_space=pl.ANY)
    return pl.pallas_call(
        body,
        name=name,
        out_shape=out_shape,
        in_specs=[smem if i in in_smem else anys if i in in_any else vmem for i in range(n_in)],
        out_specs=[smem if i in out_smem else vmem for i in range(len(out_shape))],
        scratch_shapes=list(scratch),
        compiler_params=pltpu.CompilerParams(vmem_limit_bytes=VMEM_LIMIT),
    )


def shape(dims, dtype):
    return jax.ShapeDtypeStruct(dims, dtype)


def swap(value, axis, mask):
    size = lax.axis_size(axis)
    return lax.ppermute(value, axis, [(i, i ^ mask) for i in range(size)])


def add_pair(a, b):
    return (a.astype(F32) + b.astype(F32)).astype(BF)


def shards(
    feats, cotangent, w_reduce, w_group, w_expand, scale1, shift1, scale2, shift2,
    scale3, shift3, tile_count, joined,
):
    devices = lax.axis_size("tile")
    slides = lax.axis_size("slide")
    per = MID // devices
    x, g = feats[0], cotangent[0]
    s1, b1, s2, b2 = (v.reshape(1, MID) for v in (scale1, shift1, scale2, shift2))
    s3, b3 = (v.reshape(1, CIN) for v in (scale3, shift3))

    to_core, to_other, meta = call(
        edge_kernel, "edges",
        [shape((PAY, CIN), BF), shape((PAY, CIN), BF), shape((META,), jnp.int32)],
        (0, 1), (2, 3), 4,
        [pltpu.VMEM((2, CIN, PIX), BF), pltpu.VMEM((2, CIN, PIX), BF), pltpu.SemaphoreType.DMA((4,))],
        (2,),
    )(tile_count, joined, x, g)
    from_core = swap(to_core, "tile", 1)
    hops = [(i, i + 1) for i in range(1, devices - 1, 2)]
    from_other = lax.ppermute(to_other, "tile", hops + [(b, a) for a, b in hops])

    hid, slope_a, dense, denset, wet = call(
        prep_kernel, "prep",
        [shape((SLOTS, MID, PIX), BF), shape((SLOTS, MID, PIX), F32), shape((2, HALF, KDIM), BF),
         shape((2, HALF, KDIM), BF), shape((CIN, MID), BF)],
        (0,), (), 7,
    )(meta, x, w_reduce, w_expand, w_group, s1, b1)

    out, back, errb, e_send, e_keep = call(
        functools.partial(forward_kernel, devices), "forward",
        [shape((SLOTS, CIN, PIX), BF), shape((SLOTS, CIN, PIX), F32), shape((SLOTS + 1, MID, PIX), BF),
         shape((HALF, CIN), BF), shape((HALF, CIN), BF)],
        (0,), (), 16,
        [pltpu.VMEM((SLOTS + 1, MID, PIX), BF), pltpu.VMEM((2, KDIM, (SLOTS + 1) * PIX), BF),
         pltpu.VMEM((MID, (SLOTS + 1) * PIX), BF), pltpu.VMEM((MID, (SLOTS + 1) * PIX), F32),
         pltpu.VMEM((CIN, (SLOTS + 1) * PIX), BF)],
    )(meta, from_core, from_other, hid, w_reduce, s1, b1, dense, s2, b2, wet, w_expand, s3, b3, x, g)

    e_core = swap(e_send, "tile", 1)
    erra, r_send, r_keep = call(
        functools.partial(backward_kernel, devices), "backward",
        [shape((SLOTS, MID, PIX), BF), shape((HALF, CIN + HALF), BF), shape((HALF, CIN + HALF), BF)],
        (0,), (), 6,
        [pltpu.VMEM((2, KDIM, SLOTS * PIX), BF), pltpu.VMEM((MID, SLOTS * PIX), BF), pltpu.VMEM((MID, HALF), BF)],
    )(meta, errb, hid, slope_a, denset, x)

    (grad_in,) = call(
        grad_kernel, "grads", [shape((SLOTS, CIN, PIX), BF)], (), (), 3,
    )(w_reduce, erra, back)

    quarter = HALF // 2
    e_half = add_pair(e_keep, e_core)
    e_y = swap(e_half[quarter:], "tile", 2)
    e_quarter = add_pair(e_half[:quarter], e_y)
    r_core = swap(r_send, "tile", 1)
    r_half = add_pair(r_keep, r_core)
    groups4 = [[low + 4 * k for k in range(devices // 4)] for low in range(4)]
    groups2 = [[low + 2 * k for k in range(devices // 2)] for low in range(2)]
    e_all = lax.all_to_all(e_quarter, "tile", 0, 0, axis_index_groups=groups4, tiled=True)
    r_all = lax.all_to_all(r_half, "tile", 0, 0, axis_index_groups=groups2, tiled=True)
    e_sum = jnp.sum(e_all.reshape(devices // 4, per, CIN).astype(F32), 0)
    r_sum = jnp.sum(r_all.reshape(devices // 2, per, CIN + HALF).astype(F32), 0)
    total = jnp.concatenate([e_sum, r_sum], axis=1).astype(BF)
    mask = 1
    while mask < slides:
        total = total.astype(F32) + swap(total.astype(BF), "slide", mask).astype(F32)
        mask *= 2
    norm = 1.0 / math.sqrt(slides * LIVE_DEV * devices * PIX)
    total = total.astype(F32) * norm
    grad_expand = total[:, :CIN]
    grad_reduce = total[:, CIN : 2 * CIN]
    grad_group = total[:, 2 * CIN : 2 * CIN + TAPS * GW]
    return (out[None], grad_in[None], grad_reduce, grad_group, grad_expand)


def solution(mesh):
    tiles = P("slide", "tile", None, None)
    in_specs = (tiles, tiles) + (P(),) * 9 + (P("slide", None), P("slide", None))
    out_specs = (tiles, tiles, P("tile", None), P("tile", None), P("tile", None))
    return jax.shard_map(shards, mesh=mesh, in_specs=in_specs, out_specs=out_specs, check_vma=False)
```

```python
import functools
import math

import jax
import jax.numpy as jnp
from jax import lax
from jax.experimental import pallas as pl
from jax.experimental.pallas import tpu as pltpu
from jax.sharding import PartitionSpec as P

CIN = 1024
MID = 512
GW = 16
TH = 16
TW = 8
PIX = 128
SLOTS = 4
HALF = 256
TAPS = 9
KDIM = TAPS * HALF
PAY = 48
LIVE_DEV = 2
BF = jnp.bfloat16
F32 = jnp.float32

HELD, L_LINK, R_LINK, L_IDX, R_IDX, META = 0, 1, 6, 11, 16, 24


def nt_dot(a, b):
    return lax.dot_general(a, b, (((1,), (1,)), ((), ())), preferred_element_type=F32)


def tn_dot(a, b):
    return lax.dot_general(a, b, (((0,), (0,)), ((), ())), preferred_element_type=F32)


def nn_dot(a, b):
    return lax.dot_general(a, b, (((1,), (0,)), ((), ())), preferred_element_type=F32)


def sigmoid(v):
    return 0.5 * jnp.tanh(0.5 * v) + 0.5


def column(row_ref):
    row = row_ref[...]
    return jnp.transpose(jnp.broadcast_to(row, (PIX, row.shape[1])))


def wide(col, lanes):
    return jnp.concatenate([col] * (lanes // PIX), axis=1)


def edge_select(rows, lane_of):
    row = lax.broadcasted_iota(jnp.int32, (rows, PIX), 0)
    lane = lax.broadcasted_iota(jnp.int32, (rows, PIX), 1)
    return (lane == lane_of(row)).astype(F32).astype(BF)


def x_lane(first):
    return lambda row: (row % TH) * TW + row // TH + first


def g_lane(col):
    return lambda row: row * TW + col


def edge_kernel(
    count_hbm, joined_hbm, x_any, g_any, core_ref, other_ref, meta_ref,
    count_ref, joined_ref, xbuf, gbuf, sems,
):
    me = lax.axis_index("tile")
    tables = [
        pltpu.make_async_copy(count_hbm, count_ref, sems.at[4]),
        pltpu.make_async_copy(joined_hbm, joined_ref, sems.at[5]),
    ]
    firsts = [
        pltpu.make_async_copy(x_any.at[0], xbuf.at[0], sems.at[0]),
        pltpu.make_async_copy(g_any.at[0], gbuf.at[0], sems.at[1]),
    ]
    for copy in tables + firsts:
        copy.start()
    for copy in tables:
        copy.wait()
    devices = count_ref.shape[1]
    links = joined_ref.shape[1]
    start = jnp.int32(0)
    held = jnp.int32(0)
    for e in range(devices):
        start = start + jnp.where(e < me, count_ref[0, e], 0)
        held = held + jnp.where(e == me, count_ref[0, e], 0)
    last = held - 1
    lasts = [
        pltpu.make_async_copy(x_any.at[last], xbuf.at[1], sems.at[2]),
        pltpu.make_async_copy(g_any.at[last], gbuf.at[1], sems.at[3]),
    ]
    for copy in lasts:
        copy.start()

    def link(at):
        inside = jnp.logical_and(at >= 0, at < links)
        return jnp.where(inside, joined_ref[0, jnp.clip(at, 0, links - 1)], 0)

    meta_ref[HELD] = held
    first_left = link(start - 1)
    last_right = link(start + last)
    for i in range(SLOTS):
        live = i < held
        meta_ref[L_LINK + i] = jnp.where(live, link(start + i - 1), 0)
        meta_ref[R_LINK + i] = jnp.where(live, link(start + i), 0)
        meta_ref[L_IDX + i] = jnp.int32(SLOTS if i == 0 else i - 1)
        meta_ref[R_IDX + i] = jnp.where(i >= last, SLOTS, i + 1).astype(jnp.int32)
    meta_ref[L_LINK + SLOTS] = last_right
    meta_ref[R_LINK + SLOTS] = first_left
    meta_ref[L_IDX + SLOTS] = last
    meta_ref[R_IDX + SLOTS] = jnp.int32(0)

    for copy in firsts + lasts:
        copy.wait()
    even = me % 2 == 0

    def payload(side, x_first, g_col):
        return (
            nt_dot(edge_select(2 * TH, x_lane(x_first)), xbuf[side]).astype(BF),
            nt_dot(edge_select(TH, g_lane(g_col)), gbuf[side]).astype(BF),
        )

    left_x, left_g = payload(0, 0, 0)
    right_x, right_g = payload(1, TW - 2, TW - 1)

    @pl.when(even)
    def _():
        core_ref[: 2 * TH] = right_x
        core_ref[2 * TH :] = right_g
        other_ref[: 2 * TH] = left_x
        other_ref[2 * TH :] = left_g

    @pl.when(jnp.logical_not(even))
    def _():
        core_ref[: 2 * TH] = left_x
        core_ref[2 * TH :] = left_g
        other_ref[: 2 * TH] = right_x
        other_ref[2 * TH :] = right_g


def prep_kernel(
    meta_ref, x_ref, wr_ref, we_ref, wg_ref, s1_ref, b1_ref,
    hid_ref, slope_ref, dense_ref, denset_ref, wet_ref,
):
    scale = column(s1_ref)
    shift = column(b1_ref)
    held = meta_ref[HELD]
    for half in range(SLOTS // 2):
        tiles = jnp.concatenate([x_ref[2 * half], x_ref[2 * half + 1]], axis=1)
        reduced = nn_dot(wr_ref[...], tiles)
        for k in range(2):
            i = 2 * half + k
            pre = reduced[:, k * PIX : (k + 1) * PIX] * scale + shift
            sig = sigmoid(pre)
            act = pre * sig
            hid_ref[i] = act.astype(BF)
            live = jnp.where(i < held, 1.0, 0.0).astype(F32)
            slope_ref[i] = (sig + act * (1.0 - sig)) * (scale * live)
    tap_row = lax.broadcasted_iota(jnp.int32, (TAPS * GW, KDIM), 0)
    lane = lax.broadcasted_iota(jnp.int32, (TAPS * GW, KDIM), 1)
    pick = (tap_row == (lane // HALF) * GW + lane % GW).astype(F32).astype(BF)
    spread = tn_dot(wg_ref[...], pick)
    row = lax.broadcasted_iota(jnp.int32, (MID, KDIM), 0)
    col = lax.broadcasted_iota(jnp.int32, (MID, KDIM), 1)
    keep = (row % HALF) // GW == (col % HALF) // GW
    dense_ref[...] = jnp.where(keep, spread, 0.0).astype(BF).reshape(2, HALF, KDIM)
    row_t = lax.broadcasted_iota(jnp.int32, (HALF, MID), 0)
    col_t = lax.broadcasted_iota(jnp.int32, (HALF, MID), 1)
    keep_t = row_t // GW == (col_t % HALF) // GW
    prow = lax.broadcasted_iota(jnp.int32, (HALF, TAPS * GW), 0)
    pcol = lax.broadcasted_iota(jnp.int32, (HALF, TAPS * GW), 1)
    for k in range(TAPS):
        pick_t = (pcol == k * GW + prow % GW).astype(F32).astype(BF)
        spread_t = jnp.where(keep_t, nn_dot(pick_t, wg_ref[...]), 0.0).astype(BF)
        for b in range(2):
            denset_ref[b, :, k * HALF : (k + 1) * HALF] = spread_t[:, b * HALF : (b + 1) * HALF]
    wet_ref[...] = jnp.transpose(we_ref[...])


def build_windows(field_ref, win_ref, meta_ref, tiles, transposed):
    lane = lax.broadcasted_iota(jnp.int32, (HALF, PIX), 1)
    col = lane % TW
    first_col = col == 0
    last_col = col == TW - 1
    has_above = lane >= TW
    has_below = lane < PIX - TW
    for i in tiles:
        left_at = meta_ref[L_IDX + i]
        right_at = meta_ref[R_IDX + i]
        left_link = meta_ref[L_LINK + i].astype(F32)
        right_link = meta_ref[R_LINK + i].astype(F32)
        lanes = pl.ds(i * PIX, PIX)
        for b in range(2):
            rows = pl.ds(b * HALF, HALF)
            own = field_ref[i, rows, :].astype(F32)
            left = field_ref[left_at, rows, :].astype(F32) * left_link
            right = field_ref[right_at, rows, :].astype(F32) * right_link
            west = jnp.where(first_col, pltpu.roll(left, PIX - TW + 1, 1), pltpu.roll(own, 1, 1))
            east = jnp.where(last_col, pltpu.roll(right, TW - 1, 1), pltpu.roll(own, PIX - 1, 1))
            for v, base in enumerate((west, own, east)):
                above = jnp.where(has_above, pltpu.roll(base, TW, 1), 0.0)
                below = jnp.where(has_below, pltpu.roll(base, PIX - TW, 1), 0.0)
                for u, shifted in enumerate((above, base, below)):
                    tap = 3 * u + v
                    if transposed:
                        tap = TAPS - 1 - tap
                    win_ref[b, pl.ds(tap * HALF, HALF), lanes] = shifted.astype(BF)


CHUNKS = ((0, 2), (2, 2), (4, 1))


def forward_kernel(
    devices, meta_ref, core_ref, other_ref, hid_in, wr_ref, s1_ref, b1_ref, dense_ref,
    s2_ref, b2_ref, wet_ref, s3_ref, b3_ref, x_ref, g_ref,
    out_ref, back_ref, errc_ref, slopeb_ref, send_ref, keep_ref,
    hid_ref, win_ref, hidb_ref,
):
    me = lax.axis_index("tile")
    held = meta_ref[HELD]
    odd = me % 2
    scale1 = column(s1_ref)
    shift1 = column(b1_ref)
    scale2 = column(s2_ref)
    shift2 = column(b2_ref)
    scale3 = column(s3_ref)
    shift3 = column(b3_ref)
    core_first = jnp.where(odd == 0, 0, TW - 2)
    other_first = jnp.where(odd == 0, TW - 2, 0)
    core_g = jnp.where(odd == 0, 0, TW - 1)
    other_g = jnp.where(odd == 0, TW - 1, 0)
    edge_x = (
        tn_dot(core_ref[: 2 * TH, :], edge_select(2 * TH, x_lane(core_first)))
        + tn_dot(other_ref[: 2 * TH, :], edge_select(2 * TH, x_lane(other_first)))
    ).astype(BF)
    edge_g = (
        tn_dot(core_ref[2 * TH :, :], edge_select(TH, g_lane(core_g)))
        + tn_dot(other_ref[2 * TH :, :], edge_select(TH, g_lane(other_g)))
    )
    for i in range(SLOTS):
        hid_ref[i] = hid_in[i]
    pre = nn_dot(wr_ref[...], edge_x) * scale1 + shift1
    hid_ref[SLOTS] = (pre * sigmoid(pre)).astype(BF)

    for first, count in CHUNKS:
        build_windows(hid_ref, win_ref, meta_ref, range(first, first + count), False)
        lanes = slice(first * PIX, (first + count) * PIX)
        for b in range(2):
            conv = nn_dot(dense_ref[b], win_ref[b, :, lanes])
            rows = slice(b * HALF, (b + 1) * HALF)
            for k in range(count):
                at = slice((first + k) * PIX, (first + k + 1) * PIX)
                v = conv[:, k * PIX : (k + 1) * PIX] * scale2[rows] + shift2[rows]
                sig = sigmoid(v)
                act = v * sig
                hidb_ref[rows, at] = act.astype(BF)
                slopeb_ref[rows, at] = (sig + act * (1.0 - sig)) * scale2[rows]
        grown = nn_dot(wet_ref[...], hidb_ref[:, lanes])
        for k in range(count):
            i = first + k
            if i < SLOTS:
                tile = x_ref[i].astype(F32)
                cot = g_ref[i].astype(F32)
            else:
                tile = edge_x.astype(F32)
                cot = edge_g
            total = grown[:, k * PIX : (k + 1) * PIX] * scale3 + shift3 + tile
            sig = sigmoid(total)
            act = total * sig
            back = cot * (sig + act * (1.0 - sig))
            if i < SLOTS:
                live = jnp.where(i < held, 1.0, 0.0).astype(F32)
                back = back * live
                out_ref[i] = (act * live).astype(BF)
                back_ref[i] = back
            errc_ref[:, i * PIX : (i + 1) * PIX] = (back * scale3).astype(BF)

    own = SLOTS * PIX
    for ref, flip in ((send_ref, 1), (keep_ref, 0)):
        rows = jnp.concatenate([hidb_ref[at, :own] for at in row_blocks(devices, me, flip)], axis=0)
        ref[...] = nt_dot(rows, errc_ref[:, :own]).astype(BF)


def row_blocks(devices, me, flip):
    per = MID // devices
    bits = (devices // 2).bit_length() - 1
    blocks = []
    for j in range(devices // 2):
        distance = flip
        for bit in range(bits):
            distance |= ((j >> (bits - 1 - bit)) & 1) << (bit + 1)
        at = pl.multiple_of((me ^ distance) * per, per)
        blocks.append(pl.ds(at, per))
    return blocks


def pull_kernel(we_ref, errc_ref, slopeb_ref, errb_ref):
    for first, count in CHUNKS:
        lanes = slice(first * PIX, (first + count) * PIX)
        pulled = nn_dot(we_ref[...], errc_ref[:, lanes])
        errb = (pulled * slopeb_ref[:, lanes]).astype(BF)
        for k in range(count):
            errb_ref[first + k] = errb[:, k * PIX : (k + 1) * PIX]


def backward_kernel(
    devices, meta_ref, errb_ref, hid_ref, slope_ref, denset_ref, x_ref,
    erra_ref, send_ref, keep_ref, win_ref, flat_ref, groups_ref,
):
    me = lax.axis_index("tile")
    side = lax.axis_index("slide") % 2
    for first, count in CHUNKS[:2]:
        build_windows(errb_ref, win_ref, meta_ref, range(first, first + count), True)
        lanes = slice(first * PIX, (first + count) * PIX)
        for b in range(2):
            conv = nn_dot(denset_ref[b], win_ref[b, :, lanes])
            rows = slice(b * HALF, (b + 1) * HALF)
            for k in range(count):
                i = first + k
                err = (conv[:, k * PIX : (k + 1) * PIX] * slope_ref[i, rows, :]).astype(BF)
                flat_ref[rows, i * PIX : (i + 1) * PIX] = err
                erra_ref[i, rows, :] = err
    row = lax.broadcasted_iota(jnp.int32, (HALF, HALF), 0)
    col = lax.broadcasted_iota(jnp.int32, (HALF, HALF), 1)
    same = row // GW == col // GW
    for b in range(2):
        rows = slice(b * HALF, (b + 1) * HALF)
        hid = jnp.concatenate([hid_ref[i, rows, :] for i in range(SLOTS)], axis=1)
        folded = jnp.zeros((HALF, HALF), F32)
        for k in range(TAPS):
            full = nt_dot(win_ref[b, k * HALF : (k + 1) * HALF, :], hid)
            kept = jnp.where(same, full, 0.0).astype(BF)
            place = (col == k * GW + row % GW).astype(F32).astype(BF)
            folded = folded + nn_dot(kept, place)
        groups_ref[rows, :] = folded.astype(BF)
    width = CIN // 2
    tiles = [
        jnp.concatenate([x_ref[i, pl.ds(pl.multiple_of((side ^ dx) * width, width), width), :] for i in range(SLOTS)], axis=1)
        for dx in range(2)
    ]
    for ref, flip in ((send_ref, 1), (keep_ref, 0)):
        blocks = row_blocks(devices, me, flip)
        rows = jnp.concatenate([flat_ref[at, :] for at in blocks], axis=0)
        group_rows = jnp.concatenate([groups_ref[at, :] for at in blocks], axis=0)
        low, high = group_rows[:, :PIX], group_rows[:, PIX:]
        for dx in range(2):
            ref[dx, :, :width] = nt_dot(rows, tiles[dx]).astype(BF)
            ref[dx, :, width:] = jnp.where(side == dx, low, high)


def grad_kernel(wr_ref, erra_ref, back_ref, grad_ref):
    for half in range(SLOTS // 2):
        err = jnp.concatenate([erra_ref[2 * half], erra_ref[2 * half + 1]], axis=1)
        pulled = tn_dot(wr_ref[...], err)
        for k in range(2):
            i = 2 * half + k
            grad_ref[i] = (pulled[:, k * PIX : (k + 1) * PIX] + back_ref[i]).astype(BF)


def finish_kernel(norm, e_ref, r_ref, got_ref, reduce_ref, group_ref, expand_ref):
    width = CIN // 2
    own = r_ref[...].astype(F32) * norm
    other = got_ref[:, CIN:].astype(F32) * norm
    expand_ref[...] = (e_ref[...].astype(F32) + got_ref[:, :CIN].astype(F32)) * norm
    even = lax.axis_index("slide") % 2 == 0
    low = jnp.where(even, own, other)
    high = jnp.where(even, other, own)
    reduce_ref[:, :width] = low[:, :width]
    reduce_ref[:, width:] = high[:, :width]
    group_ref[:, :PIX] = low[:, width:]
    group_ref[:, PIX:] = high[:, width : width + TAPS * GW - PIX]


LIMITS = {"edges": 3, "prep": 13, "forward": 26, "pull": 6, "backward": 16, "grads": 6, "finish": 2}
WORK = {"edges": 2, "prep": 3, "forward": 7, "pull": 1.5, "backward": 8, "grads": 2, "finish": 1}


def call(body, name, out_shape, in_smem, in_any, n_in, scratch=(), out_smem=()):
    vmem = pl.BlockSpec(memory_space=pltpu.VMEM)
    smem = pl.BlockSpec(memory_space=pltpu.SMEM)
    anys = pl.BlockSpec(memory_space=pltpu.HBM)
    return pl.pallas_call(
        body,
        name=name,
        out_shape=out_shape,
        in_specs=[smem if i in in_smem else anys if i in in_any else vmem for i in range(n_in)],
        out_specs=[smem if i in out_smem else vmem for i in range(len(out_shape))],
        scratch_shapes=list(scratch),
        compiler_params=pltpu.CompilerParams(vmem_limit_bytes=LIMITS[name] * 1024 * 1024),
        cost_estimate=pl.CostEstimate(flops=int(WORK[name] * 1.1e9), bytes_accessed=1 << 20, transcendentals=0),
    )


def shape(dims, dtype):
    return jax.ShapeDtypeStruct(dims, dtype)


def swap(value, axis, mask):
    size = lax.axis_size(axis)
    return lax.ppermute(value, axis, [(i, i ^ mask) for i in range(size)])


def cross(value, devices, slides, tile_mask, slide_mask):
    pairs = [
        (t * slides + k, (t ^ tile_mask) * slides + (k ^ slide_mask))
        for t in range(devices)
        for k in range(slides)
    ]
    return lax.ppermute(value, ("tile", "slide"), pairs)


def add_all(first, *others):
    total = first.astype(F32)
    for other in others:
        total = total + other.astype(F32)
    return total.astype(BF)


def add_pair(a, b):
    return add_all(a, b)


def halve(part, mask):
    rows = part.shape[0] // 2
    return add_pair(part[:rows], swap(part[rows:], "tile", mask))


def shards(
    feats, cotangent, w_reduce, w_group, w_expand, scale1, shift1, scale2, shift2,
    scale3, shift3, tile_count, joined,
):
    devices = lax.axis_size("tile")
    slides = lax.axis_size("slide")
    per = MID // devices
    x, g = feats[0], cotangent[0]
    s1, b1, s2, b2 = (v.reshape(1, MID) for v in (scale1, shift1, scale2, shift2))
    s3, b3 = (v.reshape(1, CIN) for v in (scale3, shift3))

    to_core, to_other, meta = call(
        edge_kernel, "edges",
        [shape((PAY, CIN), BF), shape((PAY, CIN), BF), shape((META,), jnp.int32)],
        (), (0, 1, 2, 3), 4,
        [pltpu.SMEM(tile_count.shape, jnp.int32), pltpu.SMEM(joined.shape, jnp.int32),
         pltpu.VMEM((2, CIN, PIX), BF), pltpu.VMEM((2, CIN, PIX), BF), pltpu.SemaphoreType.DMA((6,))],
        (2,),
    )(tile_count, joined, x, g)
    hops = [(i, i + 1) for i in range(1, devices - 1, 2)]
    from_other = lax.ppermute(to_other, "tile", hops + [(b, a) for a, b in hops])
    from_core = swap(to_core, "tile", 1)

    hid, slope_a, dense, denset, wet = call(
        prep_kernel, "prep",
        [shape((SLOTS, MID, PIX), BF), shape((SLOTS, MID, PIX), F32), shape((2, HALF, KDIM), BF),
         shape((2, HALF, KDIM), BF), shape((CIN, MID), BF)],
        (0,), (), 7,
    )(meta, x, w_reduce, w_expand, w_group.T, s1, b1)

    lanes = (SLOTS + 1) * PIX
    out, back, errc, slope_b, e_send, e_keep = call(
        functools.partial(forward_kernel, devices), "forward",
        [shape((SLOTS, CIN, PIX), BF), shape((SLOTS, CIN, PIX), F32), shape((CIN, lanes), BF),
         shape((MID, lanes), F32), shape((HALF, CIN), BF), shape((HALF, CIN), BF)],
        (0,), (), 15,
        [pltpu.VMEM((SLOTS + 1, MID, PIX), BF), pltpu.VMEM((2, KDIM, lanes), BF), pltpu.VMEM((MID, lanes), BF)],
    )(meta, from_core, from_other, hid, w_reduce, s1, b1, dense, s2, b2, wet, s3, b3, x, g)

    e_core = swap(e_send, "tile", 1)
    (errb,) = call(pull_kernel, "pull", [shape((SLOTS + 1, MID, PIX), BF)], (), (), 3)(w_expand, errc, slope_b)
    e_part = add_pair(e_keep, e_core)
    errb, e_part = lax.optimization_barrier((errb, e_part))
    e_part = halve(e_part, 2)

    erra, r_send, r_keep = call(
        functools.partial(backward_kernel, devices), "backward",
        [shape((SLOTS, MID, PIX), BF), shape((2, HALF, CIN // 2 + PIX), BF), shape((2, HALF, CIN // 2 + PIX), BF)],
        (0,), (), 6,
        [pltpu.VMEM((2, KDIM, SLOTS * PIX), BF), pltpu.VMEM((MID, SLOTS * PIX), BF), pltpu.VMEM((MID, HALF), BF)],
    )(meta, errb, hid, slope_a, denset, x)

    (grad_in,) = call(
        grad_kernel, "grads", [shape((SLOTS, CIN, PIX), BF)], (), (), 3,
    )(w_reduce, erra, back)

    r_core = swap(r_send, "tile", 1)
    r_part = add_pair(r_keep, r_core)
    quarter = HALF // 2
    r_part = add_all(
        r_part[0, :quarter],
        cross(r_part[0, quarter:], devices, slides, 2, 0),
        cross(r_part[1, :quarter], devices, slides, 0, 1),
        cross(r_part[1, quarter:], devices, slides, 2, 1),
    )
    mask = 4
    while mask < devices:
        e_part = halve(e_part, mask)
        r_part = halve(r_part, mask)
        mask *= 2
    mask = 2
    while mask < slides:
        e_part = add_pair(e_part, swap(e_part, "slide", mask))
        r_part = add_pair(r_part, swap(r_part, "slide", mask))
        mask *= 2
    got = swap(jnp.concatenate([e_part, r_part], axis=1), "slide", 1)
    norm = 1.0 / math.sqrt(slides * LIVE_DEV * devices * PIX)
    grad_reduce, grad_group, grad_expand = call(
        functools.partial(finish_kernel, norm), "finish",
        [shape((per, CIN), F32), shape((per, TAPS * GW), F32), shape((per, CIN), F32)], (), (), 3,
    )(e_part, r_part, got)
    return (out[None], grad_in[None], grad_reduce, grad_group, grad_expand)


def solution(mesh):
    tiles = P("slide", "tile", None, None)
    in_specs = (tiles, tiles) + (P(),) * 9 + (P("slide", None), P("slide", None))
    out_specs = (tiles, tiles, P("tile", None), P("tile", None), P("tile", None))
    return jax.shard_map(shards, mesh=mesh, in_specs=in_specs, out_specs=out_specs, check_vma=False)
```

```python
import functools
import math

import jax
import jax.numpy as jnp
import numpy as np
from jax import lax
from jax.experimental import pallas as pl
from jax.experimental.pallas import tpu as pltpu
from jax.sharding import PartitionSpec as P

CIN = 1024
MID = 512
GW = 16
TH = 16
TW = 8
PIX = 128
SLOTS = 4
HALF = 256
TAPS = 9
KDIM = TAPS * HALF
PAY = 48
LIVE_DEV = 2
BF = jnp.bfloat16
F32 = jnp.float32

HELD, L_IDX, R_IDX, META = 0, 1, 6, 16
EDGE, ZERO = SLOTS, SLOTS + 1


def nt_dot(a, b):
    return lax.dot_general(a, b, (((1,), (1,)), ((), ())), preferred_element_type=F32)


def tn_dot(a, b):
    return lax.dot_general(a, b, (((0,), (0,)), ((), ())), preferred_element_type=F32)


def nn_dot(a, b):
    return lax.dot_general(a, b, (((1,), (0,)), ((), ())), preferred_element_type=F32)


def sigmoid(v):
    return 0.5 * jnp.tanh(0.5 * v) + 0.5


def column(row_ref):
    row = row_ref[...]
    return jnp.transpose(jnp.broadcast_to(row, (PIX, row.shape[1])))


def wide(col, lanes):
    return jnp.concatenate([col] * (lanes // PIX), axis=1)


def edge_select(rows, lane_of):
    row = lax.broadcasted_iota(jnp.int32, (rows, PIX), 0)
    lane = lax.broadcasted_iota(jnp.int32, (rows, PIX), 1)
    return (lane == lane_of(row)).astype(F32).astype(BF)


def x_lane(first):
    return lambda row: (row % TH) * TW + row // TH + first


def g_lane(col):
    return lambda row: row * TW + col


def edge_kernel(
    count_hbm, joined_hbm, x_any, g_any, core_ref, other_ref, meta_ref,
    count_ref, joined_ref, xbuf, gbuf, sems,
):
    me = lax.axis_index("tile")
    tables = [
        pltpu.make_async_copy(count_hbm, count_ref, sems.at[2]),
        pltpu.make_async_copy(joined_hbm, joined_ref, sems.at[3]),
    ]
    loads = [pltpu.make_async_copy(x_any, xbuf, sems.at[0]), pltpu.make_async_copy(g_any, gbuf, sems.at[1])]
    for copy in tables + loads:
        copy.start()
    for copy in tables:
        copy.wait()
    devices = count_ref.shape[1]
    links = joined_ref.shape[1]
    start = jnp.int32(0)
    held = jnp.int32(0)
    for e in range(devices):
        start = start + jnp.where(e < me, count_ref[0, e], 0)
        held = held + jnp.where(e == me, count_ref[0, e], 0)
    last = held - 1
    def joined_to(at, neighbour):
        inside = jnp.logical_and(at >= 0, at < links)
        on = joined_ref[0, jnp.clip(at, 0, links - 1)] != 0
        return jnp.where(jnp.logical_and(inside, on), neighbour, ZERO).astype(jnp.int32)

    meta_ref[HELD] = held
    for i in range(SLOTS):
        left = joined_to(start + i - 1, EDGE if i == 0 else i - 1)
        right = joined_to(start + i, jnp.where(i >= last, EDGE, i + 1))
        meta_ref[L_IDX + i] = jnp.where(i < held, left, ZERO).astype(jnp.int32)
        meta_ref[R_IDX + i] = jnp.where(i < held, right, ZERO).astype(jnp.int32)
    meta_ref[L_IDX + EDGE] = joined_to(start + last, last)
    meta_ref[R_IDX + EDGE] = joined_to(start - 1, 0)

    for copy in loads:
        copy.wait()
    even = me % 2 == 0

    def payload(slot, x_first, g_col):
        return (
            nt_dot(edge_select(2 * TH, x_lane(x_first)), xbuf[slot]).astype(BF),
            nt_dot(edge_select(TH, g_lane(g_col)), gbuf[slot]).astype(BF),
        )

    left_x, left_g = payload(0, 0, 0)
    right_x, right_g = payload(last, TW - 2, TW - 1)

    @pl.when(even)
    def _():
        core_ref[: 2 * TH] = right_x
        core_ref[2 * TH :] = right_g
        other_ref[: 2 * TH] = left_x
        other_ref[2 * TH :] = left_g

    @pl.when(jnp.logical_not(even))
    def _():
        core_ref[: 2 * TH] = left_x
        core_ref[2 * TH :] = left_g
        other_ref[: 2 * TH] = right_x
        other_ref[2 * TH :] = right_g


def prep_kernel(
    meta_ref, x_ref, wr_ref, we_ref, wg_ref, s1_ref, b1_ref,
    hid_ref, slope_ref, dense_ref, denset_ref, wet_ref,
):
    scale = column(s1_ref)
    shift = column(b1_ref)
    held = meta_ref[HELD]
    for half in range(SLOTS // 2):
        tiles = jnp.concatenate([x_ref[2 * half], x_ref[2 * half + 1]], axis=1)
        reduced = nn_dot(wr_ref[...], tiles)
        for k in range(2):
            i = 2 * half + k
            pre = reduced[:, k * PIX : (k + 1) * PIX] * scale + shift
            sig = sigmoid(pre)
            act = pre * sig
            hid_ref[i] = act.astype(BF)
            live = jnp.where(i < held, 1.0, 0.0).astype(F32)
            slope_ref[i] = (sig + act * (1.0 - sig)) * (scale * live)
    tap_row = lax.broadcasted_iota(jnp.int32, (TAPS * GW, KDIM), 0)
    lane = lax.broadcasted_iota(jnp.int32, (TAPS * GW, KDIM), 1)
    pick = (tap_row == (lane // HALF) * GW + lane % GW).astype(F32).astype(BF)
    spread = tn_dot(wg_ref[...], pick)
    row = lax.broadcasted_iota(jnp.int32, (MID, KDIM), 0)
    col = lax.broadcasted_iota(jnp.int32, (MID, KDIM), 1)
    keep = (row % HALF) // GW == (col % HALF) // GW
    dense_ref[...] = jnp.where(keep, spread, 0.0).astype(BF).reshape(2, HALF, KDIM)
    row_t = lax.broadcasted_iota(jnp.int32, (HALF, MID), 0)
    col_t = lax.broadcasted_iota(jnp.int32, (HALF, MID), 1)
    keep_t = row_t // GW == (col_t % HALF) // GW
    prow = lax.broadcasted_iota(jnp.int32, (HALF, TAPS * GW), 0)
    pcol = lax.broadcasted_iota(jnp.int32, (HALF, TAPS * GW), 1)
    for k in range(TAPS):
        pick_t = (pcol == k * GW + prow % GW).astype(F32).astype(BF)
        spread_t = jnp.where(keep_t, nn_dot(pick_t, wg_ref[...]), 0.0).astype(BF)
        for b in range(2):
            denset_ref[b, :, k * HALF : (k + 1) * HALF] = spread_t[:, b * HALF : (b + 1) * HALF]
    wet_ref[...] = jnp.transpose(we_ref[...])


def silu_slope(v):
    sig = sigmoid(v)
    act = v * sig
    return act, sig + act * (1.0 - sig)


def build_windows(field_ref, win_ref, meta_ref, tiles, first, transposed):
    lane = lax.broadcasted_iota(jnp.int32, (HALF, PIX), 1)
    col = lane % TW
    first_col = col == 0
    last_col = col == TW - 1
    has_above = lane >= TW
    has_below = lane < PIX - TW
    zero = jnp.zeros((), BF)
    for i in tiles:
        left_at = meta_ref[L_IDX + i]
        right_at = meta_ref[R_IDX + i]
        lanes = pl.ds((i - first) * PIX, PIX)
        for b in range(2):
            rows = pl.ds(b * HALF, HALF)
            own = field_ref[i, rows, :]
            left = field_ref[left_at, rows, :]
            right = field_ref[right_at, rows, :]
            west = jnp.where(first_col, pltpu.roll(left, PIX - TW + 1, 1), pltpu.roll(own, 1, 1))
            east = jnp.where(last_col, pltpu.roll(right, TW - 1, 1), pltpu.roll(own, PIX - 1, 1))
            for v, base in enumerate((west, own, east)):
                above = jnp.where(has_above, pltpu.roll(base, TW, 1), zero)
                below = jnp.where(has_below, pltpu.roll(base, PIX - TW, 1), zero)
                for u, shifted in enumerate((above, base, below)):
                    tap = 3 * u + v
                    if transposed:
                        tap = TAPS - 1 - tap
                    win_ref[b, pl.ds(tap * HALF, HALF), lanes] = shifted


CHUNKS = ((0, 2), (2, 2))


def forward_kernel(
    devices, meta_ref, core_ref, other_ref, hid_in, wr_ref, s1_ref, b1_ref, dense_ref,
    s2_ref, b2_ref, wet_ref, s3_ref, b3_ref, x_ref, g_ref,
    out_ref, back_ref, errc_ref, slopeb_ref, hid_ref, edge_ref, send_ref, keep_ref,
    win_ref, hidb_ref,
):
    me = lax.axis_index("tile")
    held = meta_ref[HELD]
    odd = me % 2
    scale1 = column(s1_ref)
    shift1 = column(b1_ref)
    scale2 = column(s2_ref)
    shift2 = column(b2_ref)
    scale3 = column(s3_ref)
    shift3 = column(b3_ref)
    core_first = jnp.where(odd == 0, 0, TW - 2)
    other_first = jnp.where(odd == 0, TW - 2, 0)
    edge_x = (
        tn_dot(core_ref[: 2 * TH, :], edge_select(2 * TH, x_lane(core_first)))
        + tn_dot(other_ref[: 2 * TH, :], edge_select(2 * TH, x_lane(other_first)))
    ).astype(BF)
    edge_ref[...] = edge_x
    for i in range(SLOTS):
        hid_ref[i] = hid_in[i]
    pre = nn_dot(wr_ref[...], edge_x) * scale1 + shift1
    hid_ref[EDGE] = (pre * sigmoid(pre)).astype(BF)
    hid_ref[ZERO] = jnp.zeros((MID, PIX), BF)

    for first, count in CHUNKS:
        build_windows(hid_ref, win_ref, meta_ref, range(first, first + count), 0, False)
        lanes = slice(first * PIX, (first + count) * PIX)
        for b in range(2):
            conv = nn_dot(dense_ref[b], win_ref[b, :, lanes])
            rows = slice(b * HALF, (b + 1) * HALF)
            for k in range(count):
                at = slice((first + k) * PIX, (first + k + 1) * PIX)
                act, slope = silu_slope(conv[:, k * PIX : (k + 1) * PIX] * scale2[rows] + shift2[rows])
                hidb_ref[rows, at] = act.astype(BF)
                slopeb_ref[rows, at] = slope * scale2[rows]
        grown = nn_dot(wet_ref[...], hidb_ref[:, lanes])
        for k in range(count):
            i = first + k
            act, slope = silu_slope(
                grown[:, k * PIX : (k + 1) * PIX] * scale3 + shift3 + x_ref[i].astype(F32)
            )
            live = jnp.where(i < held, 1.0, 0.0).astype(F32)
            back = g_ref[i].astype(F32) * slope * live
            out_ref[i] = (act * live).astype(BF)
            back_ref[i] = back
            errc_ref[:, i * PIX : (i + 1) * PIX] = (back * scale3).astype(BF)

    own = SLOTS * PIX
    for ref, flip in ((send_ref, 1), (keep_ref, 0)):
        rows = jnp.concatenate([hidb_ref[at, :own] for at in row_blocks(devices, me, flip)], axis=0)
        ref[...] = nt_dot(rows, errc_ref[:, :own]).astype(BF)


def row_blocks(devices, me, flip):
    per = MID // devices
    bits = (devices // 2).bit_length() - 1
    blocks = []
    for j in range(devices // 2):
        distance = flip
        for bit in range(bits):
            distance |= ((j >> (bits - 1 - bit)) & 1) << (bit + 1)
        at = pl.multiple_of((me ^ distance) * per, per)
        blocks.append(pl.ds(at, per))
    return blocks


def pull_kernel(
    meta_ref, core_ref, other_ref, hid_ref, dense_ref, s2_ref, b2_ref, wet_ref, s3_ref, b3_ref,
    edge_ref, we_ref, errc_ref, slopeb_ref, errb_ref, win_ref, hidb_ref, slope_ref,
):
    odd = lax.axis_index("tile") % 2
    core_g = jnp.where(odd == 0, 0, TW - 1)
    other_g = jnp.where(odd == 0, TW - 1, 0)
    edge_g = (
        tn_dot(core_ref[2 * TH :, :], edge_select(TH, g_lane(core_g)))
        + tn_dot(other_ref[2 * TH :, :], edge_select(TH, g_lane(other_g)))
    )
    scale2 = column(s2_ref)
    shift2 = column(b2_ref)
    scale3 = column(s3_ref)
    shift3 = column(b3_ref)
    build_windows(hid_ref, win_ref, meta_ref, (EDGE,), EDGE, False)
    for b in range(2):
        conv = nn_dot(dense_ref[b], win_ref[b])
        rows = slice(b * HALF, (b + 1) * HALF)
        act, slope = silu_slope(conv * scale2[rows] + shift2[rows])
        hidb_ref[rows, :] = act.astype(BF)
        slope_ref[rows, :] = slope * scale2[rows]
    for first, count in CHUNKS:
        lanes = slice(first * PIX, (first + count) * PIX)
        pulled = nn_dot(we_ref[...], errc_ref[:, lanes])
        errb = (pulled * slopeb_ref[:, lanes]).astype(BF)
        for k in range(count):
            errb_ref[first + k] = errb[:, k * PIX : (k + 1) * PIX]
    grown = nn_dot(wet_ref[...], hidb_ref[...])
    _, slope = silu_slope(grown * scale3 + shift3 + edge_ref[...].astype(F32))
    errc = (edge_g * slope * scale3).astype(BF)
    errb_ref[EDGE] = (nn_dot(we_ref[...], errc) * slope_ref[...]).astype(BF)
    errb_ref[ZERO] = jnp.zeros((MID, PIX), BF)


def backward_kernel(
    devices, meta_ref, errb_ref, hid_ref, slope_ref, denset_ref, x_ref, place_ref,
    erra_ref, *rest,
):
    send_refs, keep_refs = rest[:4], rest[4:8]
    win_ref, flat_ref, groups_ref, kept_ref = rest[8:]
    me = lax.axis_index("tile")
    side = lax.axis_index("slide") % 2
    for first, count in CHUNKS:
        build_windows(errb_ref, win_ref, meta_ref, range(first, first + count), 0, True)
        lanes = slice(first * PIX, (first + count) * PIX)
        for b in range(2):
            conv = nn_dot(denset_ref[b], win_ref[b, :, lanes])
            rows = slice(b * HALF, (b + 1) * HALF)
            for k in range(count):
                i = first + k
                err = (conv[:, k * PIX : (k + 1) * PIX] * slope_ref[i, rows, :]).astype(BF)
                flat_ref[rows, i * PIX : (i + 1) * PIX] = err
                erra_ref[i, rows, :] = err
    row = lax.broadcasted_iota(jnp.int32, (HALF, HALF), 0)
    col = lax.broadcasted_iota(jnp.int32, (HALF, HALF), 1)
    same = row // GW == col // GW
    for b in range(2):
        rows = slice(b * HALF, (b + 1) * HALF)
        hid = jnp.transpose(jnp.concatenate([hid_ref[i, rows, :] for i in range(SLOTS)], axis=1))
        for k in range(TAPS):
            full = nn_dot(win_ref[b, k * HALF : (k + 1) * HALF, :], hid)
            kept_ref[:, k * HALF : (k + 1) * HALF] = jnp.where(same, full, 0.0).astype(BF)
        groups_ref[rows, :] = nn_dot(kept_ref[...], place_ref[...]).astype(BF)
    width = CIN // 2
    tiles = [
        jnp.concatenate([x_ref[i, pl.ds(pl.multiple_of((side ^ dx) * width, width), width), :] for i in range(SLOTS)], axis=1)
        for dx in range(2)
    ]
    quarter = HALF // 2
    for refs, flip in ((send_refs, 1), (keep_refs, 0)):
        blocks = row_blocks(devices, me, flip)
        rows = jnp.concatenate([flat_ref[at, :] for at in blocks], axis=0)
        group_rows = jnp.concatenate([groups_ref[at, :] for at in blocks], axis=0)
        low, high = group_rows[:, :PIX], group_rows[:, PIX:]
        for dx in range(2):
            part = nt_dot(rows, tiles[dx]).astype(BF)
            group_part = jnp.where(side == dx, low, high)
            for dy in range(2):
                at = slice(dy * quarter, (dy + 1) * quarter)
                refs[2 * dx + dy][:, :width] = part[at]
                refs[2 * dx + dy][:, width:] = group_part[at]


def grad_kernel(wr_ref, erra_ref, back_ref, act_ref, grad_ref, out_ref):
    out_ref[...] = act_ref[...]
    for half in range(SLOTS // 2):
        err = jnp.concatenate([erra_ref[2 * half], erra_ref[2 * half + 1]], axis=1)
        pulled = tn_dot(wr_ref[...], err)
        for k in range(2):
            i = 2 * half + k
            grad_ref[i] = (pulled[:, k * PIX : (k + 1) * PIX] + back_ref[i]).astype(BF)


def finish_kernel(norm, e_ref, r_ref, got_ref, reduce_ref, group_ref, expand_ref):
    width = CIN // 2
    own = r_ref[...].astype(F32) * norm
    other = got_ref[:, CIN:].astype(F32) * norm
    expand_ref[...] = (e_ref[...].astype(F32) + got_ref[:, :CIN].astype(F32)) * norm
    even = lax.axis_index("slide") % 2 == 0
    low = jnp.where(even, own, other)
    high = jnp.where(even, other, own)
    reduce_ref[:, :width] = low[:, :width]
    reduce_ref[:, width:] = high[:, :width]
    group_ref[:, :PIX] = low[:, width:]
    group_ref[:, PIX:] = high[:, width : width + TAPS * GW - PIX]


LIMITS = {"edges": 56, "prep": 13, "forward": 26, "pull": 14, "backward": 18, "grads": 9, "finish": 2}
WORK = {"edges": 2, "prep": 3, "forward": 7, "pull": 2, "backward": 5, "grads": 2, "finish": 1}


def call(body, name, out_shape, in_smem, in_any, n_in, scratch=(), out_smem=()):
    vmem = pl.BlockSpec(memory_space=pltpu.VMEM)
    smem = pl.BlockSpec(memory_space=pltpu.SMEM)
    anys = pl.BlockSpec(memory_space=pltpu.HBM)
    return pl.pallas_call(
        body,
        name=name,
        out_shape=out_shape,
        in_specs=[smem if i in in_smem else anys if i in in_any else vmem for i in range(n_in)],
        out_specs=[smem if i in out_smem else vmem for i in range(len(out_shape))],
        scratch_shapes=list(scratch),
        compiler_params=pltpu.CompilerParams(vmem_limit_bytes=LIMITS[name] * 1024 * 1024),
        cost_estimate=pl.CostEstimate(flops=int(WORK[name] * 1.1e9), bytes_accessed=1 << 20, transcendentals=0),
    )


def shape(dims, dtype):
    return jax.ShapeDtypeStruct(dims, dtype)


def swap(value, axis, mask):
    size = lax.axis_size(axis)
    return lax.ppermute(value, axis, [(i, i ^ mask) for i in range(size)])


def tap_places():
    row = np.arange(KDIM)
    place = np.zeros((KDIM, HALF), np.float32)
    place[row, row // HALF * GW + row % GW] = 1.0
    return jnp.asarray(place, BF)


def cross(value, devices, slides, tile_mask, slide_mask):
    pairs = [
        (t * slides + k, (t ^ tile_mask) * slides + (k ^ slide_mask))
        for t in range(devices)
        for k in range(slides)
    ]
    return lax.ppermute(value, ("tile", "slide"), pairs)


def add_all(first, *others):
    total = first.astype(F32)
    for other in others:
        total = total + other.astype(F32)
    return total.astype(BF)


def add_pair(a, b):
    return add_all(a, b)


def halve(part, mask):
    rows = part.shape[0] // 2
    return add_pair(part[:rows], swap(part[rows:], "tile", mask))


def shards(
    feats, cotangent, w_reduce, w_group, w_expand, scale1, shift1, scale2, shift2,
    scale3, shift3, tile_count, joined,
):
    devices = lax.axis_size("tile")
    slides = lax.axis_size("slide")
    per = MID // devices
    x, g = feats[0], cotangent[0]
    s1, b1, s2, b2 = (v.reshape(1, MID) for v in (scale1, shift1, scale2, shift2))
    s3, b3 = (v.reshape(1, CIN) for v in (scale3, shift3))

    to_core, to_other, meta = call(
        edge_kernel, "edges",
        [shape((PAY, CIN), BF), shape((PAY, CIN), BF), shape((META,), jnp.int32)],
        (), (0, 1, 2, 3), 4,
        [pltpu.SMEM(tile_count.shape, jnp.int32), pltpu.SMEM(joined.shape, jnp.int32),
         pltpu.VMEM((SLOTS, CIN, PIX), BF), pltpu.VMEM((SLOTS, CIN, PIX), BF), pltpu.SemaphoreType.DMA((4,))],
        (2,),
    )(tile_count, joined, x, g)
    hops = [(i, i + 1) for i in range(1, devices - 1, 2)]
    from_other = lax.ppermute(to_other, "tile", hops + [(b, a) for a, b in hops])
    from_core = swap(to_core, "tile", 1)

    hid, slope_a, dense, denset, wet = call(
        prep_kernel, "prep",
        [shape((SLOTS, MID, PIX), BF), shape((SLOTS, MID, PIX), F32), shape((2, HALF, KDIM), BF),
         shape((2, HALF, KDIM), BF), shape((CIN, MID), BF)],
        (0,), (), 7,
    )(meta, x, w_reduce, w_expand, w_group.T, s1, b1)

    lanes = SLOTS * PIX
    act, back, errc, slope_b, hid, edge, e_send, e_keep = call(
        functools.partial(forward_kernel, devices), "forward",
        [shape((SLOTS, CIN, PIX), BF), shape((SLOTS, CIN, PIX), F32), shape((CIN, lanes), BF),
         shape((MID, lanes), F32), shape((SLOTS + 2, MID, PIX), BF), shape((CIN, PIX), BF),
         shape((HALF, CIN), BF), shape((HALF, CIN), BF)],
        (0,), (), 15,
        [pltpu.VMEM((2, KDIM, lanes), BF), pltpu.VMEM((MID, lanes), BF)],
    )(meta, from_core, from_other, hid, w_reduce, s1, b1, dense, s2, b2, wet, s3, b3, x, g)

    e_core = swap(e_send, "tile", 1)
    (errb,) = call(
        pull_kernel, "pull", [shape((SLOTS + 2, MID, PIX), BF)], (0,), (), 14,
        [pltpu.VMEM((2, KDIM, PIX), BF), pltpu.VMEM((MID, PIX), BF), pltpu.VMEM((MID, PIX), F32)],
    )(meta, from_core, from_other, hid, dense, s2, b2, wet, s3, b3, edge, w_expand, errc, slope_b)
    e_part = add_pair(e_keep, e_core)
    errb, e_part = lax.optimization_barrier((errb, e_part))
    e_part = halve(e_part, 2)

    piece = [shape((HALF // 2, CIN // 2 + PIX), BF)] * 8
    erra, *pieces = call(
        functools.partial(backward_kernel, devices), "backward", [shape((SLOTS, MID, PIX), BF)] + piece,
        (0,), (), 7,
        [pltpu.VMEM((2, KDIM, lanes), BF), pltpu.VMEM((MID, lanes), BF), pltpu.VMEM((MID, HALF), BF),
         pltpu.VMEM((HALF, KDIM), BF)],
    )(meta, errb, hid, slope_a, denset, x, tap_places())
    (grad_in, out) = call(
        grad_kernel, "grads", [shape((SLOTS, CIN, PIX), BF), shape((SLOTS, CIN, PIX), BF)], (), (), 4,
    )(w_reduce, erra, back, act)

    r_core = [swap(value, "tile", 1) for value in pieces[:4]]
    *r_core, e_part = lax.optimization_barrier((*r_core, e_part))
    near, far_y, far_x, far_xy = (add_pair(a, b) for a, b in zip(pieces[4:], r_core))
    one = cross(far_y, devices, slides, 2, 0)
    two = cross(far_x, devices, slides, 0, 1)
    three = cross(far_xy, devices, slides, 2, 1)
    mask = 4
    while mask < devices:
        if 2 * mask == devices:
            e_part, two = lax.optimization_barrier((e_part, two))
        e_part = halve(e_part, mask)
        mask *= 2
    r_part = add_all(near, one, two, three)
    mask = 4
    while mask < devices:
        r_part = halve(r_part, mask)
        mask *= 2
    mask = 2
    while mask < slides:
        e_part = add_pair(e_part, swap(e_part, "slide", mask))
        r_part = add_pair(r_part, swap(r_part, "slide", mask))
        mask *= 2
    got = swap(jnp.concatenate([e_part, r_part], axis=1), "slide", 1)
    norm = 1.0 / math.sqrt(slides * LIVE_DEV * devices * PIX)
    grad_reduce, grad_group, grad_expand = call(
        functools.partial(finish_kernel, norm), "finish",
        [shape((per, CIN), F32), shape((per, TAPS * GW), F32), shape((per, CIN), F32)], (), (), 3,
    )(e_part, r_part, got)
    return (out[None], grad_in[None], grad_reduce, grad_group, grad_expand)


def solution(mesh):
    tiles = P("slide", "tile", None, None)
    in_specs = (tiles, tiles) + (P(),) * 9 + (P("slide", None), P("slide", None))
    out_specs = (tiles, tiles, P("tile", None), P("tile", None), P("tile", None))
    return jax.shard_map(shards, mesh=mesh, in_specs=in_specs, out_specs=out_specs, check_vma=False)
```

```python
import functools
import math

import jax
import jax.numpy as jnp
import numpy as np
from jax import lax
from jax.experimental import pallas as pl
from jax.experimental.pallas import tpu as pltpu
from jax.sharding import PartitionSpec as P

CIN = 1024
MID = 512
GW = 16
TH = 16
TW = 8
PIX = 128
SLOTS = 4
HALF = 256
TAPS = 9
KDIM = TAPS * HALF
PAY = 48
LIVE_DEV = 2
BF = jnp.bfloat16
F32 = jnp.float32

HELD, L_IDX, R_IDX, META = 0, 1, 6, 16
EDGE, ZERO = SLOTS, SLOTS + 1


def nt_dot(a, b):
    return lax.dot_general(a, b, (((1,), (1,)), ((), ())), preferred_element_type=F32)


def tn_dot(a, b):
    return lax.dot_general(a, b, (((0,), (0,)), ((), ())), preferred_element_type=F32)


def nn_dot(a, b):
    return lax.dot_general(a, b, (((1,), (0,)), ((), ())), preferred_element_type=F32)


def sigmoid(v):
    return 0.5 * jnp.tanh(0.5 * v) + 0.5


def column(row_ref):
    row = row_ref[...]
    return jnp.transpose(jnp.broadcast_to(row, (PIX, row.shape[1])))


def wide(col, lanes):
    return jnp.concatenate([col] * (lanes // PIX), axis=1)


def edge_select(rows, lane_of):
    row = lax.broadcasted_iota(jnp.int32, (rows, PIX), 0)
    lane = lax.broadcasted_iota(jnp.int32, (rows, PIX), 1)
    return (lane == lane_of(row)).astype(F32).astype(BF)


def x_lane(first):
    return lambda row: (row % TH) * TW + row // TH + first


def g_lane(col):
    return lambda row: row * TW + col


def edge_kernel(
    count_hbm, joined_hbm, x_any, g_any, core_ref, other_ref, meta_ref,
    count_ref, joined_ref, xbuf, gbuf, sems,
):
    me = lax.axis_index("tile")
    tables = [
        pltpu.make_async_copy(count_hbm, count_ref, sems.at[2]),
        pltpu.make_async_copy(joined_hbm, joined_ref, sems.at[3]),
    ]
    loads = [pltpu.make_async_copy(x_any, xbuf, sems.at[0]), pltpu.make_async_copy(g_any, gbuf, sems.at[1])]
    for copy in tables + loads:
        copy.start()
    for copy in tables:
        copy.wait()
    devices = count_ref.shape[1]
    links = joined_ref.shape[1]
    start = jnp.int32(0)
    held = jnp.int32(0)
    for e in range(devices):
        start = start + jnp.where(e < me, count_ref[0, e], 0)
        held = held + jnp.where(e == me, count_ref[0, e], 0)
    last = held - 1
    def joined_to(at, neighbour):
        inside = jnp.logical_and(at >= 0, at < links)
        on = joined_ref[0, jnp.clip(at, 0, links - 1)] != 0
        return jnp.where(jnp.logical_and(inside, on), neighbour, ZERO).astype(jnp.int32)

    meta_ref[HELD] = held
    for i in range(SLOTS):
        left = joined_to(start + i - 1, EDGE if i == 0 else i - 1)
        right = joined_to(start + i, jnp.where(i >= last, EDGE, i + 1))
        meta_ref[L_IDX + i] = jnp.where(i < held, left, ZERO).astype(jnp.int32)
        meta_ref[R_IDX + i] = jnp.where(i < held, right, ZERO).astype(jnp.int32)
    meta_ref[L_IDX + EDGE] = joined_to(start + last, last)
    meta_ref[R_IDX + EDGE] = joined_to(start - 1, 0)

    for copy in loads:
        copy.wait()
    even = me % 2 == 0

    def payload(slot, x_first, g_col):
        return (
            nt_dot(edge_select(2 * TH, x_lane(x_first)), xbuf[slot]).astype(BF),
            nt_dot(edge_select(TH, g_lane(g_col)), gbuf[slot]).astype(BF),
        )

    left_x, left_g = payload(0, 0, 0)
    right_x, right_g = payload(last, TW - 2, TW - 1)

    @pl.when(even)
    def _():
        core_ref[: 2 * TH] = right_x
        core_ref[2 * TH :] = right_g
        other_ref[: 2 * TH] = left_x
        other_ref[2 * TH :] = left_g

    @pl.when(jnp.logical_not(even))
    def _():
        core_ref[: 2 * TH] = left_x
        core_ref[2 * TH :] = left_g
        other_ref[: 2 * TH] = right_x
        other_ref[2 * TH :] = right_g


def prep_kernel(
    meta_ref, x_ref, wr_ref, we_ref, wg_ref, s1_ref, b1_ref,
    hid_ref, slope_ref, dense_ref, denset_ref, wet_ref,
):
    scale = column(s1_ref)
    shift = column(b1_ref)
    held = meta_ref[HELD]
    for half in range(SLOTS // 2):
        tiles = jnp.concatenate([x_ref[2 * half], x_ref[2 * half + 1]], axis=1)
        reduced = nn_dot(wr_ref[...], tiles)
        for k in range(2):
            i = 2 * half + k
            pre = reduced[:, k * PIX : (k + 1) * PIX] * scale + shift
            sig = sigmoid(pre)
            act = pre * sig
            hid_ref[i] = act.astype(BF)
            live = jnp.where(i < held, 1.0, 0.0).astype(F32)
            slope_ref[i] = (sig + act * (1.0 - sig)) * (scale * live)
    tap_row = lax.broadcasted_iota(jnp.int32, (TAPS * GW, KDIM), 0)
    lane = lax.broadcasted_iota(jnp.int32, (TAPS * GW, KDIM), 1)
    pick = (tap_row == (lane // HALF) * GW + lane % GW).astype(F32).astype(BF)
    spread = tn_dot(wg_ref[...], pick)
    row = lax.broadcasted_iota(jnp.int32, (MID, KDIM), 0)
    col = lax.broadcasted_iota(jnp.int32, (MID, KDIM), 1)
    keep = (row % HALF) // GW == (col % HALF) // GW
    dense_ref[...] = jnp.where(keep, spread, 0.0).astype(BF).reshape(2, HALF, KDIM)
    row_t = lax.broadcasted_iota(jnp.int32, (HALF, MID), 0)
    col_t = lax.broadcasted_iota(jnp.int32, (HALF, MID), 1)
    keep_t = row_t // GW == (col_t % HALF) // GW
    prow = lax.broadcasted_iota(jnp.int32, (HALF, TAPS * GW), 0)
    pcol = lax.broadcasted_iota(jnp.int32, (HALF, TAPS * GW), 1)
    for k in range(TAPS):
        pick_t = (pcol == k * GW + prow % GW).astype(F32).astype(BF)
        spread_t = jnp.where(keep_t, nn_dot(pick_t, wg_ref[...]), 0.0).astype(BF)
        for b in range(2):
            denset_ref[b, :, k * HALF : (k + 1) * HALF] = spread_t[:, b * HALF : (b + 1) * HALF]
    wet_ref[...] = jnp.transpose(we_ref[...])


def silu_slope(v):
    sig = sigmoid(v)
    act = v * sig
    return act, sig + act * (1.0 - sig)


def build_windows(field_ref, win_ref, meta_ref, tiles, first, transposed):
    lane = lax.broadcasted_iota(jnp.int32, (HALF, PIX), 1)
    col = lane % TW
    first_col = col == 0
    last_col = col == TW - 1
    has_above = lane >= TW
    has_below = lane < PIX - TW
    zero = jnp.zeros((), BF)
    for i in tiles:
        left_at = meta_ref[L_IDX + i]
        right_at = meta_ref[R_IDX + i]
        lanes = pl.ds((i - first) * PIX, PIX)
        for b in range(2):
            rows = pl.ds(b * HALF, HALF)
            own = field_ref[i, rows, :]
            left = field_ref[left_at, rows, :]
            right = field_ref[right_at, rows, :]
            west = jnp.where(first_col, pltpu.roll(left, PIX - TW + 1, 1), pltpu.roll(own, 1, 1))
            east = jnp.where(last_col, pltpu.roll(right, TW - 1, 1), pltpu.roll(own, PIX - 1, 1))
            for v, base in enumerate((west, own, east)):
                above = jnp.where(has_above, pltpu.roll(base, TW, 1), zero)
                below = jnp.where(has_below, pltpu.roll(base, PIX - TW, 1), zero)
                for u, shifted in enumerate((above, base, below)):
                    tap = 3 * u + v
                    if transposed:
                        tap = TAPS - 1 - tap
                    win_ref[b, pl.ds(tap * HALF, HALF), lanes] = shifted


CHUNKS = ((0, 2), (2, 2))


def forward_kernel(
    devices, meta_ref, core_ref, other_ref, hid_in, wr_ref, s1_ref, b1_ref, dense_ref,
    s2_ref, b2_ref, wet_ref, s3_ref, b3_ref, x_ref, g_ref,
    out_ref, back_ref, errc_ref, slopeb_ref, hid_ref, edge_ref, send_ref, keep_ref,
    win_ref, hidb_ref,
):
    me = lax.axis_index("tile")
    held = meta_ref[HELD]
    odd = me % 2
    scale1 = column(s1_ref)
    shift1 = column(b1_ref)
    scale2 = column(s2_ref)
    shift2 = column(b2_ref)
    scale3 = column(s3_ref)
    shift3 = column(b3_ref)
    core_first = jnp.where(odd == 0, 0, TW - 2)
    other_first = jnp.where(odd == 0, TW - 2, 0)
    edge_x = (
        tn_dot(core_ref[: 2 * TH, :], edge_select(2 * TH, x_lane(core_first)))
        + tn_dot(other_ref[: 2 * TH, :], edge_select(2 * TH, x_lane(other_first)))
    ).astype(BF)
    edge_ref[...] = edge_x
    for i in range(SLOTS):
        hid_ref[i] = hid_in[i]
    pre = nn_dot(wr_ref[...], edge_x) * scale1 + shift1
    hid_ref[EDGE] = (pre * sigmoid(pre)).astype(BF)
    hid_ref[ZERO] = jnp.zeros((MID, PIX), BF)

    for first, count in CHUNKS:
        build_windows(hid_ref, win_ref, meta_ref, range(first, first + count), 0, False)
        lanes = slice(first * PIX, (first + count) * PIX)
        for b in range(2):
            conv = nn_dot(dense_ref[b], win_ref[b, :, lanes])
            rows = slice(b * HALF, (b + 1) * HALF)
            for k in range(count):
                at = slice((first + k) * PIX, (first + k + 1) * PIX)
                act, slope = silu_slope(conv[:, k * PIX : (k + 1) * PIX] * scale2[rows] + shift2[rows])
                hidb_ref[rows, at] = act.astype(BF)
                slopeb_ref[rows, at] = slope * scale2[rows]
        grown = nn_dot(wet_ref[...], hidb_ref[:, lanes])
        for k in range(count):
            i = first + k
            act, slope = silu_slope(
                grown[:, k * PIX : (k + 1) * PIX] * scale3 + shift3 + x_ref[i].astype(F32)
            )
            live = jnp.where(i < held, 1.0, 0.0).astype(F32)
            back = g_ref[i].astype(F32) * slope * live
            out_ref[i] = (act * live).astype(BF)
            back_ref[i] = back
            errc_ref[:, i * PIX : (i + 1) * PIX] = (back * scale3).astype(BF)

    own = SLOTS * PIX
    for ref, flip in ((send_ref, 1), (keep_ref, 0)):
        rows = jnp.concatenate([hidb_ref[at, :own] for at in row_blocks(devices, me, flip)], axis=0)
        ref[...] = nt_dot(rows, errc_ref[:, :own]).astype(BF)


def row_blocks(devices, me, flip):
    per = MID // devices
    bits = (devices // 2).bit_length() - 1
    blocks = []
    for j in range(devices // 2):
        distance = flip
        for bit in range(bits):
            distance |= ((j >> (bits - 1 - bit)) & 1) << (bit + 1)
        at = pl.multiple_of((me ^ distance) * per, per)
        blocks.append(pl.ds(at, per))
    return blocks


def pull_kernel(
    meta_ref, core_ref, other_ref, hid_ref, dense_ref, s2_ref, b2_ref, wet_ref, s3_ref, b3_ref,
    edge_ref, we_ref, errc_ref, slopeb_ref, errb_ref, win_ref, hidb_ref, slope_ref,
):
    odd = lax.axis_index("tile") % 2
    core_g = jnp.where(odd == 0, 0, TW - 1)
    other_g = jnp.where(odd == 0, TW - 1, 0)
    edge_g = (
        tn_dot(core_ref[2 * TH :, :], edge_select(TH, g_lane(core_g)))
        + tn_dot(other_ref[2 * TH :, :], edge_select(TH, g_lane(other_g)))
    )
    scale2 = column(s2_ref)
    shift2 = column(b2_ref)
    scale3 = column(s3_ref)
    shift3 = column(b3_ref)
    build_windows(hid_ref, win_ref, meta_ref, (EDGE,), EDGE, False)
    for b in range(2):
        conv = nn_dot(dense_ref[b], win_ref[b])
        rows = slice(b * HALF, (b + 1) * HALF)
        act, slope = silu_slope(conv * scale2[rows] + shift2[rows])
        hidb_ref[rows, :] = act.astype(BF)
        slope_ref[rows, :] = slope * scale2[rows]
    for first, count in CHUNKS:
        lanes = slice(first * PIX, (first + count) * PIX)
        pulled = nn_dot(we_ref[...], errc_ref[:, lanes])
        errb = (pulled * slopeb_ref[:, lanes]).astype(BF)
        for k in range(count):
            errb_ref[first + k] = errb[:, k * PIX : (k + 1) * PIX]
    grown = nn_dot(wet_ref[...], hidb_ref[...])
    _, slope = silu_slope(grown * scale3 + shift3 + edge_ref[...].astype(F32))
    errc = (edge_g * slope * scale3).astype(BF)
    errb_ref[EDGE] = (nn_dot(we_ref[...], errc) * slope_ref[...]).astype(BF)
    errb_ref[ZERO] = jnp.zeros((MID, PIX), BF)


def backward_kernel(
    devices, meta_ref, errb_ref, hid_ref, slope_ref, denset_ref, x_ref, place_ref,
    erra_ref, *rest,
):
    send_refs, keep_refs = rest[:4], rest[4:8]
    win_ref, flat_ref, groups_ref, kept_ref = rest[8:]
    me = lax.axis_index("tile")
    for first, count in CHUNKS:
        build_windows(errb_ref, win_ref, meta_ref, range(first, first + count), 0, True)
        lanes = slice(first * PIX, (first + count) * PIX)
        for b in range(2):
            conv = nn_dot(denset_ref[b], win_ref[b, :, lanes])
            rows = slice(b * HALF, (b + 1) * HALF)
            for k in range(count):
                i = first + k
                err = (conv[:, k * PIX : (k + 1) * PIX] * slope_ref[i, rows, :]).astype(BF)
                flat_ref[rows, i * PIX : (i + 1) * PIX] = err
                erra_ref[i, rows, :] = err
    row = lax.broadcasted_iota(jnp.int32, (HALF, HALF), 0)
    col = lax.broadcasted_iota(jnp.int32, (HALF, HALF), 1)
    same = row // GW == col // GW
    for b in range(2):
        rows = slice(b * HALF, (b + 1) * HALF)
        hid = jnp.transpose(jnp.concatenate([hid_ref[i, rows, :] for i in range(SLOTS)], axis=1))
        for k in range(TAPS):
            full = nn_dot(win_ref[b, k * HALF : (k + 1) * HALF, :], hid)
            kept_ref[:, k * HALF : (k + 1) * HALF] = jnp.where(same, full, 0.0).astype(BF)
        groups_ref[rows, :] = nn_dot(kept_ref[...], place_ref[...]).astype(BF)
    tiles = jnp.concatenate([x_ref[i] for i in range(SLOTS)], axis=1)
    count = HALF // 4
    for refs, flip in ((send_refs, 1), (keep_refs, 0)):
        blocks = row_blocks(devices, me, flip)
        rows = jnp.concatenate([flat_ref[at, :] for at in blocks], axis=0)
        group_rows = jnp.concatenate([groups_ref[at, :] for at in blocks], axis=0)
        part = nt_dot(rows, tiles).astype(BF)
        for k in range(4):
            at = slice(k * count, (k + 1) * count)
            refs[k][:, :CIN] = part[at]
            refs[k][:, CIN:] = group_rows[at]


def grad_kernel(wr_ref, erra_ref, back_ref, act_ref, grad_ref, out_ref):
    out_ref[...] = act_ref[...]
    for half in range(SLOTS // 2):
        err = jnp.concatenate([erra_ref[2 * half], erra_ref[2 * half + 1]], axis=1)
        pulled = tn_dot(wr_ref[...], err)
        for k in range(2):
            i = 2 * half + k
            grad_ref[i] = (pulled[:, k * PIX : (k + 1) * PIX] + back_ref[i]).astype(BF)


def finish_kernel(norm, ea_ref, eb_ref, *refs):
    parts, (reduce_ref, group_ref, expand_ref) = refs[:4], refs[4:]
    expand_ref[...] = (ea_ref[...].astype(F32) + eb_ref[...].astype(F32)) * norm
    total = sum(part[...].astype(F32) for part in parts) * norm
    reduce_ref[...] = total[:, :CIN]
    group_ref[...] = total[:, CIN : CIN + TAPS * GW]


LIMITS = {"edges": 56, "prep": 13, "forward": 26, "pull": 14, "backward": 18, "grads": 9, "finish": 2}
WORK = {"edges": 2, "prep": 3, "forward": 7, "pull": 2, "backward": 5, "grads": 2, "finish": 1}


def call(body, name, out_shape, in_smem, in_any, n_in, scratch=(), out_smem=()):
    vmem = pl.BlockSpec(memory_space=pltpu.VMEM)
    smem = pl.BlockSpec(memory_space=pltpu.SMEM)
    anys = pl.BlockSpec(memory_space=pltpu.HBM)
    return pl.pallas_call(
        body,
        name=name,
        out_shape=out_shape,
        in_specs=[smem if i in in_smem else anys if i in in_any else vmem for i in range(n_in)],
        out_specs=[smem if i in out_smem else vmem for i in range(len(out_shape))],
        scratch_shapes=list(scratch),
        compiler_params=pltpu.CompilerParams(vmem_limit_bytes=LIMITS[name] * 1024 * 1024),
        cost_estimate=pl.CostEstimate(flops=int(WORK[name] * 1.1e9), bytes_accessed=1 << 20, transcendentals=0),
    )


def shape(dims, dtype):
    return jax.ShapeDtypeStruct(dims, dtype)


def swap(value, axis, mask):
    size = lax.axis_size(axis)
    return lax.ppermute(value, axis, [(i, i ^ mask) for i in range(size)])


def tap_places():
    row = np.arange(KDIM)
    place = np.zeros((KDIM, HALF), np.float32)
    place[row, row // HALF * GW + row % GW] = 1.0
    return jnp.asarray(place, BF)


def cross(value, devices, slides, tile_mask, slide_mask):
    pairs = [
        (t * slides + k, (t ^ tile_mask) * slides + (k ^ slide_mask))
        for t in range(devices)
        for k in range(slides)
    ]
    return lax.ppermute(value, ("tile", "slide"), pairs)


def spread(part, devices, slides):
    rows = part.shape[0] // 4
    return [part[:rows]] + [
        cross(part[k * rows : (k + 1) * rows], devices, slides, 2 * (k // 2 + 2 * (k % 2)), 0) for k in (1, 2, 3)
    ]


def add_all(first, *others):
    total = first.astype(F32)
    for other in others:
        total = total + other.astype(F32)
    return total.astype(BF)


def add_pair(a, b):
    return add_all(a, b)


def halve(part, mask):
    rows = part.shape[0] // 2
    return add_pair(part[:rows], swap(part[rows:], "tile", mask))


def shards(
    feats, cotangent, w_reduce, w_group, w_expand, scale1, shift1, scale2, shift2,
    scale3, shift3, tile_count, joined,
):
    devices = lax.axis_size("tile")
    slides = lax.axis_size("slide")
    per = MID // devices
    x, g = feats[0], cotangent[0]
    s1, b1, s2, b2 = (v.reshape(1, MID) for v in (scale1, shift1, scale2, shift2))
    s3, b3 = (v.reshape(1, CIN) for v in (scale3, shift3))

    to_core, to_other, meta = call(
        edge_kernel, "edges",
        [shape((PAY, CIN), BF), shape((PAY, CIN), BF), shape((META,), jnp.int32)],
        (), (0, 1, 2, 3), 4,
        [pltpu.SMEM(tile_count.shape, jnp.int32), pltpu.SMEM(joined.shape, jnp.int32),
         pltpu.VMEM((SLOTS, CIN, PIX), BF), pltpu.VMEM((SLOTS, CIN, PIX), BF), pltpu.SemaphoreType.DMA((4,))],
        (2,),
    )(tile_count, joined, x, g)
    hops = [(i, i + 1) for i in range(1, devices - 1, 2)]
    from_other = lax.ppermute(to_other, "tile", hops + [(b, a) for a, b in hops])
    from_core = swap(to_core, "tile", 1)

    hid, slope_a, dense, denset, wet = call(
        prep_kernel, "prep",
        [shape((SLOTS, MID, PIX), BF), shape((SLOTS, MID, PIX), F32), shape((2, HALF, KDIM), BF),
         shape((2, HALF, KDIM), BF), shape((CIN, MID), BF)],
        (0,), (), 7,
    )(meta, x, w_reduce, w_expand, w_group.T, s1, b1)

    lanes = SLOTS * PIX
    act, back, errc, slope_b, hid, edge, e_send, e_keep = call(
        functools.partial(forward_kernel, devices), "forward",
        [shape((SLOTS, CIN, PIX), BF), shape((SLOTS, CIN, PIX), F32), shape((CIN, lanes), BF),
         shape((MID, lanes), F32), shape((SLOTS + 2, MID, PIX), BF), shape((CIN, PIX), BF),
         shape((HALF, CIN), BF), shape((HALF, CIN), BF)],
        (0,), (), 15,
        [pltpu.VMEM((2, KDIM, lanes), BF), pltpu.VMEM((MID, lanes), BF)],
    )(meta, from_core, from_other, hid, w_reduce, s1, b1, dense, s2, b2, wet, s3, b3, x, g)

    e_core = swap(e_send, "tile", 1)
    (errb,) = call(
        pull_kernel, "pull", [shape((SLOTS + 2, MID, PIX), BF)], (0,), (), 14,
        [pltpu.VMEM((2, KDIM, PIX), BF), pltpu.VMEM((MID, PIX), BF), pltpu.VMEM((MID, PIX), F32)],
    )(meta, from_core, from_other, hid, dense, s2, b2, wet, s3, b3, edge, w_expand, errc, slope_b)
    e_part = add_pair(e_keep, e_core)
    errb, e_part = lax.optimization_barrier((errb, e_part))
    e_part = halve(e_part, 2)

    piece = [shape((HALF // 4, CIN + HALF), BF)] * 8
    erra, *pieces = call(
        functools.partial(backward_kernel, devices), "backward", [shape((SLOTS, MID, PIX), BF)] + piece,
        (0,), (), 7,
        [pltpu.VMEM((2, KDIM, lanes), BF), pltpu.VMEM((MID, lanes), BF), pltpu.VMEM((MID, HALF), BF),
         pltpu.VMEM((HALF, KDIM), BF)],
    )(meta, errb, hid, slope_a, denset, x, tap_places())
    (grad_in, out) = call(
        grad_kernel, "grads", [shape((SLOTS, CIN, PIX), BF), shape((SLOTS, CIN, PIX), BF)], (), (), 4,
    )(w_reduce, erra, back, act)

    r_core = [swap(value, "tile", 1) for value in pieces[:4]]
    *r_core, e_part = lax.optimization_barrier((*r_core, e_part))
    r_parts = [add_pair(a, b) for a, b in zip(pieces[4:], r_core)]
    r_parts = [r_parts[0]] + [cross(r_parts[k], devices, slides, 2 * (k // 2 + 2 * (k % 2)), 0) for k in (1, 2, 3)]
    mask = 4
    while mask < devices:
        e_part = halve(e_part, mask)
        mask *= 2
    r_part = add_all(*r_parts)
    mask = 8
    while 2 * mask < devices:
        r_part = halve(r_part, mask)
        mask *= 2
    mine, theirs = r_part[:per], r_part[per:]
    both = cross(jnp.concatenate([mine, e_part], axis=1), devices, slides, 0, 1)
    e_other = both[:, CIN + HALF :]
    finals = [
        mine,
        both[:, : CIN + HALF],
        cross(theirs, devices, slides, devices // 2, 0),
        cross(theirs, devices, slides, devices // 2, 1),
    ]
    if slides > 2:
        e_part, e_other = add_pair(e_part, e_other), jnp.zeros_like(e_part)
        total = add_all(*finals)
        mask = 2
        while mask < slides:
            e_part = add_pair(e_part, swap(e_part, "slide", mask))
            total = add_pair(total, swap(total, "slide", mask))
            mask *= 2
        finals = [total] + [jnp.zeros_like(total)] * 3
    norm = 1.0 / math.sqrt(slides * LIVE_DEV * devices * PIX)
    grad_reduce, grad_group, grad_expand = call(
        functools.partial(finish_kernel, norm), "finish",
        [shape((per, CIN), F32), shape((per, TAPS * GW), F32), shape((per, CIN), F32)], (), (), 6,
    )(e_part, e_other, *finals)
    return (out[None], grad_in[None], grad_reduce, grad_group, grad_expand)


def solution(mesh):
    tiles = P("slide", "tile", None, None)
    in_specs = (tiles, tiles) + (P(),) * 9 + (P("slide", None), P("slide", None))
    out_specs = (tiles, tiles, P("tile", None), P("tile", None), P("tile", None))
    return jax.shard_map(shards, mesh=mesh, in_specs=in_specs, out_specs=out_specs, check_vma=False)
```

```python
import functools
import math

import jax
import jax.numpy as jnp
import numpy as np
from jax import lax
from jax.experimental import pallas as pl
from jax.experimental.pallas import tpu as pltpu
from jax.sharding import PartitionSpec as P

CIN = 1024
MID = 512
GW = 16
TH = 16
TW = 8
PIX = 128
SLOTS = 4
HALF = 256
TAPS = 9
KDIM = TAPS * HALF
PAY = 48
LIVE_DEV = 2
BF = jnp.bfloat16
F32 = jnp.float32

HELD, L_IDX, R_IDX, META = 0, 1, 6, 16
EDGE, ZERO = SLOTS, SLOTS + 1


def nt_dot(a, b):
    return lax.dot_general(a, b, (((1,), (1,)), ((), ())), preferred_element_type=F32)


def tn_dot(a, b):
    return lax.dot_general(a, b, (((0,), (0,)), ((), ())), preferred_element_type=F32)


def nn_dot(a, b):
    return lax.dot_general(a, b, (((1,), (0,)), ((), ())), preferred_element_type=F32)


def sigmoid(v):
    return 0.5 * jnp.tanh(0.5 * v) + 0.5


def column(row_ref):
    row = row_ref[...]
    return jnp.transpose(jnp.broadcast_to(row, (PIX, row.shape[1])))


def wide(col, lanes):
    return jnp.concatenate([col] * (lanes // PIX), axis=1)


def edge_select(rows, lane_of):
    row = lax.broadcasted_iota(jnp.int32, (rows, PIX), 0)
    lane = lax.broadcasted_iota(jnp.int32, (rows, PIX), 1)
    return (lane == lane_of(row)).astype(F32).astype(BF)


def x_lane(first):
    return lambda row: (row % TH) * TW + row // TH + first


def g_lane(col):
    return lambda row: row * TW + col


def edge_kernel(
    count_hbm, joined_hbm, x_any, g_any, core_ref, other_ref, meta_ref,
    count_ref, joined_ref, xbuf, gbuf, sems,
):
    me = lax.axis_index("tile")
    tables = [
        pltpu.make_async_copy(count_hbm, count_ref, sems.at[2]),
        pltpu.make_async_copy(joined_hbm, joined_ref, sems.at[3]),
    ]
    loads = [pltpu.make_async_copy(x_any, xbuf, sems.at[0]), pltpu.make_async_copy(g_any, gbuf, sems.at[1])]
    for copy in tables + loads:
        copy.start()
    for copy in tables:
        copy.wait()
    devices = count_ref.shape[1]
    links = joined_ref.shape[1]
    start = jnp.int32(0)
    held = jnp.int32(0)
    for e in range(devices):
        start = start + jnp.where(e < me, count_ref[0, e], 0)
        held = held + jnp.where(e == me, count_ref[0, e], 0)
    last = held - 1
    def joined_to(at, neighbour):
        inside = jnp.logical_and(at >= 0, at < links)
        on = joined_ref[0, jnp.clip(at, 0, links - 1)] != 0
        return jnp.where(jnp.logical_and(inside, on), neighbour, ZERO).astype(jnp.int32)

    meta_ref[HELD] = held
    for i in range(SLOTS):
        left = joined_to(start + i - 1, EDGE if i == 0 else i - 1)
        right = joined_to(start + i, jnp.where(i >= last, EDGE, i + 1))
        meta_ref[L_IDX + i] = jnp.where(i < held, left, ZERO).astype(jnp.int32)
        meta_ref[R_IDX + i] = jnp.where(i < held, right, ZERO).astype(jnp.int32)
    meta_ref[L_IDX + EDGE] = joined_to(start + last, last)
    meta_ref[R_IDX + EDGE] = joined_to(start - 1, 0)

    for copy in loads:
        copy.wait()
    even = me % 2 == 0

    def payload(slot, x_first, g_col):
        return (
            nt_dot(edge_select(2 * TH, x_lane(x_first)), xbuf[slot]).astype(BF),
            nt_dot(edge_select(TH, g_lane(g_col)), gbuf[slot]).astype(BF),
        )

    left_x, left_g = payload(0, 0, 0)
    right_x, right_g = payload(last, TW - 2, TW - 1)

    @pl.when(even)
    def _():
        core_ref[: 2 * TH] = right_x
        core_ref[2 * TH :] = right_g
        other_ref[: 2 * TH] = left_x
        other_ref[2 * TH :] = left_g

    @pl.when(jnp.logical_not(even))
    def _():
        core_ref[: 2 * TH] = left_x
        core_ref[2 * TH :] = left_g
        other_ref[: 2 * TH] = right_x
        other_ref[2 * TH :] = right_g


def prep_kernel(
    meta_ref, x_ref, wr_ref, we_ref, wg_ref, s1_ref, b1_ref,
    hid_ref, slope_ref, dense_ref, denset_ref, wet_ref,
):
    scale = column(s1_ref)
    shift = column(b1_ref)
    held = meta_ref[HELD]
    for half in range(SLOTS // 2):
        tiles = jnp.concatenate([x_ref[2 * half], x_ref[2 * half + 1]], axis=1)
        reduced = nn_dot(wr_ref[...], tiles)
        for k in range(2):
            i = 2 * half + k
            pre = reduced[:, k * PIX : (k + 1) * PIX] * scale + shift
            sig = sigmoid(pre)
            act = pre * sig
            hid_ref[i] = act.astype(BF)
            live = jnp.where(i < held, 1.0, 0.0).astype(F32)
            slope_ref[i] = (sig + act * (1.0 - sig)) * (scale * live)
    tap_row = lax.broadcasted_iota(jnp.int32, (TAPS * GW, KDIM), 0)
    lane = lax.broadcasted_iota(jnp.int32, (TAPS * GW, KDIM), 1)
    pick = (tap_row == (lane // HALF) * GW + lane % GW).astype(F32).astype(BF)
    spread = tn_dot(wg_ref[...], pick)
    row = lax.broadcasted_iota(jnp.int32, (MID, KDIM), 0)
    col = lax.broadcasted_iota(jnp.int32, (MID, KDIM), 1)
    keep = (row % HALF) // GW == (col % HALF) // GW
    dense_ref[...] = jnp.where(keep, spread, 0.0).astype(BF).reshape(2, HALF, KDIM)
    row_t = lax.broadcasted_iota(jnp.int32, (HALF, MID), 0)
    col_t = lax.broadcasted_iota(jnp.int32, (HALF, MID), 1)
    keep_t = row_t // GW == (col_t % HALF) // GW
    prow = lax.broadcasted_iota(jnp.int32, (HALF, TAPS * GW), 0)
    pcol = lax.broadcasted_iota(jnp.int32, (HALF, TAPS * GW), 1)
    for k in range(TAPS):
        pick_t = (pcol == k * GW + prow % GW).astype(F32).astype(BF)
        spread_t = jnp.where(keep_t, nn_dot(pick_t, wg_ref[...]), 0.0).astype(BF)
        for b in range(2):
            denset_ref[b, :, k * HALF : (k + 1) * HALF] = spread_t[:, b * HALF : (b + 1) * HALF]
    wet_ref[...] = jnp.transpose(we_ref[...])


def silu_slope(v):
    sig = sigmoid(v)
    act = v * sig
    return act, sig + act * (1.0 - sig)


def build_windows(field_ref, win_ref, meta_ref, tiles, first, transposed):
    lane = lax.broadcasted_iota(jnp.int32, (HALF, PIX), 1)
    col = lane % TW
    first_col = col == 0
    last_col = col == TW - 1
    has_above = lane >= TW
    has_below = lane < PIX - TW
    zero = jnp.zeros((), BF)
    for i in tiles:
        left_at = meta_ref[L_IDX + i]
        right_at = meta_ref[R_IDX + i]
        lanes = pl.ds((i - first) * PIX, PIX)
        for b in range(2):
            rows = pl.ds(b * HALF, HALF)
            own = field_ref[i, rows, :]
            left = field_ref[left_at, rows, :]
            right = field_ref[right_at, rows, :]
            west = jnp.where(first_col, pltpu.roll(left, PIX - TW + 1, 1), pltpu.roll(own, 1, 1))
            east = jnp.where(last_col, pltpu.roll(right, TW - 1, 1), pltpu.roll(own, PIX - 1, 1))
            for v, base in enumerate((west, own, east)):
                above = jnp.where(has_above, pltpu.roll(base, TW, 1), zero)
                below = jnp.where(has_below, pltpu.roll(base, PIX - TW, 1), zero)
                for u, shifted in enumerate((above, base, below)):
                    tap = 3 * u + v
                    if transposed:
                        tap = TAPS - 1 - tap
                    win_ref[b, pl.ds(tap * HALF, HALF), lanes] = shifted


CHUNKS = ((0, 2), (2, 2))


def forward_kernel(
    devices, meta_ref, core_ref, other_ref, hid_in, wr_ref, s1_ref, b1_ref, dense_ref,
    s2_ref, b2_ref, wet_ref, s3_ref, b3_ref, x_ref, g_ref,
    out_ref, back_ref, errc_ref, slopeb_ref, hid_ref, edge_ref, hide_ref, slopee_ref, send_ref, keep_ref,
    win_ref, wine_ref, hidb_ref,
):
    me = lax.axis_index("tile")
    held = meta_ref[HELD]
    odd = me % 2
    scale1 = column(s1_ref)
    shift1 = column(b1_ref)
    scale2 = column(s2_ref)
    shift2 = column(b2_ref)
    scale3 = column(s3_ref)
    shift3 = column(b3_ref)
    core_first = jnp.where(odd == 0, 0, TW - 2)
    other_first = jnp.where(odd == 0, TW - 2, 0)
    edge_x = (
        tn_dot(core_ref[: 2 * TH, :], edge_select(2 * TH, x_lane(core_first)))
        + tn_dot(other_ref[: 2 * TH, :], edge_select(2 * TH, x_lane(other_first)))
    ).astype(BF)
    edge_ref[...] = edge_x
    for i in range(SLOTS):
        hid_ref[i] = hid_in[i]
    pre = nn_dot(wr_ref[...], edge_x) * scale1 + shift1
    hid_ref[EDGE] = (pre * sigmoid(pre)).astype(BF)
    hid_ref[ZERO] = jnp.zeros((MID, PIX), BF)

    build_windows(hid_ref, wine_ref, meta_ref, (EDGE,), EDGE, False)
    for b in range(2):
        rows = slice(b * HALF, (b + 1) * HALF)
        act, slope = silu_slope(nn_dot(dense_ref[b], wine_ref[b]) * scale2[rows] + shift2[rows])
        hide_ref[rows, :] = act.astype(BF)
        slopee_ref[rows, :] = slope * scale2[rows]

    for first, count in CHUNKS:
        build_windows(hid_ref, win_ref, meta_ref, range(first, first + count), 0, False)
        lanes = slice(first * PIX, (first + count) * PIX)
        for b in range(2):
            conv = nn_dot(dense_ref[b], win_ref[b, :, lanes])
            rows = slice(b * HALF, (b + 1) * HALF)
            for k in range(count):
                at = slice((first + k) * PIX, (first + k + 1) * PIX)
                act, slope = silu_slope(conv[:, k * PIX : (k + 1) * PIX] * scale2[rows] + shift2[rows])
                hidb_ref[rows, at] = act.astype(BF)
                slopeb_ref[rows, at] = slope * scale2[rows]
        grown = nn_dot(wet_ref[...], hidb_ref[:, lanes])
        for k in range(count):
            i = first + k
            act, slope = silu_slope(
                grown[:, k * PIX : (k + 1) * PIX] * scale3 + shift3 + x_ref[i].astype(F32)
            )
            live = jnp.where(i < held, 1.0, 0.0).astype(F32)
            back = g_ref[i].astype(F32) * slope * live
            out_ref[i] = (act * live).astype(BF)
            back_ref[i] = back
            errc_ref[:, i * PIX : (i + 1) * PIX] = (back * scale3).astype(BF)

    own = SLOTS * PIX
    for ref, flip in ((send_ref, 1), (keep_ref, 0)):
        rows = jnp.concatenate([hidb_ref[at, :own] for at in row_blocks(devices, me, flip)], axis=0)
        part = nt_dot(rows, errc_ref[:, :own]).astype(BF)
        per = MID // devices
        for j in range(devices // 2):
            for c in range(CIN // PIX):
                ref[j, c * per : (c + 1) * per, :] = part[j * per : (j + 1) * per, c * PIX : (c + 1) * PIX]


def row_blocks(devices, me, flip):
    per = MID // devices
    bits = (devices // 2).bit_length() - 1
    blocks = []
    for j in range(devices // 2):
        distance = flip
        for bit in range(bits):
            distance |= ((j >> (bits - 1 - bit)) & 1) << (bit + 1)
        at = pl.multiple_of((me ^ distance) * per, per)
        blocks.append(pl.ds(at, per))
    return blocks


def pull_kernel(
    core_ref, other_ref, hide_ref, slopee_ref, wet_ref, s3_ref, b3_ref,
    edge_ref, we_ref, errc_ref, slopeb_ref, errb_ref,
):
    odd = lax.axis_index("tile") % 2
    core_g = jnp.where(odd == 0, 0, TW - 1)
    other_g = jnp.where(odd == 0, TW - 1, 0)
    edge_g = (
        tn_dot(core_ref[2 * TH :, :], edge_select(TH, g_lane(core_g)))
        + tn_dot(other_ref[2 * TH :, :], edge_select(TH, g_lane(other_g)))
    )
    scale3 = column(s3_ref)
    shift3 = column(b3_ref)
    for first, count in CHUNKS:
        lanes = slice(first * PIX, (first + count) * PIX)
        pulled = nn_dot(we_ref[...], errc_ref[:, lanes])
        errb = (pulled * slopeb_ref[:, lanes]).astype(BF)
        for k in range(count):
            errb_ref[first + k] = errb[:, k * PIX : (k + 1) * PIX]
    grown = nn_dot(wet_ref[...], hide_ref[...])
    _, slope = silu_slope(grown * scale3 + shift3 + edge_ref[...].astype(F32))
    errc = (edge_g * slope * scale3).astype(BF)
    errb_ref[EDGE] = (nn_dot(we_ref[...], errc) * slopee_ref[...]).astype(BF)
    errb_ref[ZERO] = jnp.zeros((MID, PIX), BF)


def backward_kernel(
    devices, meta_ref, errb_ref, hid_ref, slope_ref, denset_ref, x_ref, place_ref,
    erra_ref, *rest,
):
    send_refs, keep_refs = rest[:4], rest[4:8]
    win_ref, flat_ref, groups_ref, kept_ref = rest[8:]
    me = lax.axis_index("tile")
    for first, count in CHUNKS:
        build_windows(errb_ref, win_ref, meta_ref, range(first, first + count), 0, True)
        lanes = slice(first * PIX, (first + count) * PIX)
        for b in range(2):
            conv = nn_dot(denset_ref[b], win_ref[b, :, lanes])
            rows = slice(b * HALF, (b + 1) * HALF)
            for k in range(count):
                i = first + k
                err = (conv[:, k * PIX : (k + 1) * PIX] * slope_ref[i, rows, :]).astype(BF)
                flat_ref[rows, i * PIX : (i + 1) * PIX] = err
                erra_ref[i, rows, :] = err
    row = lax.broadcasted_iota(jnp.int32, (HALF, HALF), 0)
    col = lax.broadcasted_iota(jnp.int32, (HALF, HALF), 1)
    same = row // GW == col // GW
    for b in range(2):
        rows = slice(b * HALF, (b + 1) * HALF)
        hid = jnp.transpose(jnp.concatenate([hid_ref[i, rows, :] for i in range(SLOTS)], axis=1))
        for k in range(TAPS):
            full = nn_dot(win_ref[b, k * HALF : (k + 1) * HALF, :], hid)
            kept_ref[:, k * HALF : (k + 1) * HALF] = jnp.where(same, full, 0.0).astype(BF)
        groups_ref[rows, :] = nn_dot(kept_ref[...], place_ref[...]).astype(BF)
    tiles = jnp.concatenate([x_ref[i] for i in range(SLOTS)], axis=1)
    per = MID // devices
    inner = devices // 8
    lane = lax.broadcasted_iota(jnp.int32, (HALF, PIX), 1)
    row = lax.broadcasted_iota(jnp.int32, (HALF, PIX), 0)
    own_lanes = lane // GW == row % 8
    lane = lax.broadcasted_iota(jnp.int32, (PIX, PIX), 1)
    row = lax.broadcasted_iota(jnp.int32, (PIX, PIX), 0)
    repeat = (lane % GW == row).astype(F32).astype(BF)
    pack = lax.broadcasted_iota(jnp.int32, (4 * devices, HALF), 0)
    row = lax.broadcasted_iota(jnp.int32, (4 * devices, HALF), 1)
    gather = jnp.logical_and(pack // 8 == row // per, pack % 8 == (row % per) // 8).astype(F32).astype(BF)
    for refs, flip in ((send_refs, 1), (keep_refs, 0)):
        blocks = row_blocks(devices, me, flip)
        rows = jnp.concatenate([flat_ref[at, :] for at in blocks], axis=0)
        group_rows = jnp.concatenate([groups_ref[at, :] for at in blocks], axis=0)
        part = nt_dot(rows, tiles).astype(BF)
        tail = jnp.where(own_lanes, nn_dot(group_rows[:, PIX:], repeat), 0.0).astype(BF)
        tail = nn_dot(gather, tail).astype(BF)
        for j in range(devices // 2):
            ref, i = refs[j // inner], j % inner
            at = slice(j * per, (j + 1) * per)
            for c in range(CIN // PIX):
                ref[i, c * per : (c + 1) * per, :] = part[at, c * PIX : (c + 1) * PIX]
            ref[i, 8 * per : 9 * per, :] = group_rows[at, :PIX]
            ref[i, 9 * per :, :] = tail[8 * j : 8 * j + 8]


def grad_kernel(wr_ref, erra_ref, back_ref, act_ref, grad_ref, out_ref):
    out_ref[...] = act_ref[...]
    for half in range(SLOTS // 2):
        err = jnp.concatenate([erra_ref[2 * half], erra_ref[2 * half + 1]], axis=1)
        pulled = tn_dot(wr_ref[...], err)
        for k in range(2):
            i = 2 * half + k
            grad_ref[i] = (pulled[:, k * PIX : (k + 1) * PIX] + back_ref[i]).astype(BF)


def finish_kernel(norm, ea_ref, eb_ref, *refs):
    parts, (reduce_ref, group_ref, expand_ref) = refs[:4], refs[4:]
    expand = (ea_ref[...].astype(F32) + eb_ref[...].astype(F32)) * norm
    total = sum(part[...].astype(F32) for part in parts) * norm
    per = reduce_ref.shape[0]
    for c in range(CIN // PIX):
        reduce_ref[:, c * PIX : (c + 1) * PIX] = total[c * per : (c + 1) * per]
        expand_ref[:, c * PIX : (c + 1) * PIX] = expand[c * per : (c + 1) * per]
    group_ref[:, :PIX] = total[8 * per : 9 * per]
    tail = jnp.concatenate(
        [jnp.broadcast_to(total[9 * per + k : 9 * per + k + 1], (8, PIX)) for k in range(per // 8)], axis=0
    )
    lane = lax.broadcasted_iota(jnp.int32, (per, PIX), 1)
    row = lax.broadcasted_iota(jnp.int32, (per, PIX), 0)
    tail = jnp.where(lane // GW == row % 8, tail, 0.0)
    for shift in (64, 32, 16):
        tail = tail + pltpu.roll(tail, shift, 1)
    group_ref[:, PIX:] = tail[:, : TAPS * GW - PIX]


LIMITS = {"edges": 56, "prep": 13, "forward": 26, "pull": 11, "backward": 18, "grads": 9, "finish": 2}
WORK = {"edges": 2, "prep": 3, "forward": 7, "pull": 2, "backward": 5, "grads": 2, "finish": 1}


def call(body, name, out_shape, in_smem, in_any, n_in, scratch=(), out_smem=()):
    vmem = pl.BlockSpec(memory_space=pltpu.VMEM)
    smem = pl.BlockSpec(memory_space=pltpu.SMEM)
    anys = pl.BlockSpec(memory_space=pltpu.HBM)
    return pl.pallas_call(
        body,
        name=name,
        out_shape=out_shape,
        in_specs=[smem if i in in_smem else anys if i in in_any else vmem for i in range(n_in)],
        out_specs=[smem if i in out_smem else vmem for i in range(len(out_shape))],
        scratch_shapes=list(scratch),
        compiler_params=pltpu.CompilerParams(vmem_limit_bytes=LIMITS[name] * 1024 * 1024),
        cost_estimate=pl.CostEstimate(flops=int(WORK[name] * 1.1e9), bytes_accessed=1 << 20, transcendentals=0),
    )


def shape(dims, dtype):
    return jax.ShapeDtypeStruct(dims, dtype)


def swap(value, axis, mask):
    size = lax.axis_size(axis)
    return lax.ppermute(value, axis, [(i, i ^ mask) for i in range(size)])


def tap_places():
    row = np.arange(KDIM)
    place = np.zeros((KDIM, HALF), np.float32)
    place[row, row // HALF * GW + row % GW] = 1.0
    return jnp.asarray(place, BF)


def cross(value, devices, slides, tile_mask, slide_mask):
    pairs = [
        (t * slides + k, (t ^ tile_mask) * slides + (k ^ slide_mask))
        for t in range(devices)
        for k in range(slides)
    ]
    return lax.ppermute(value, ("tile", "slide"), pairs)


def spread(part, devices, slides):
    rows = part.shape[0] // 4
    return [part[:rows]] + [
        cross(part[k * rows : (k + 1) * rows], devices, slides, 2 * (k // 2 + 2 * (k % 2)), 0) for k in (1, 2, 3)
    ]


def add_all(first, *others):
    total = first.astype(F32)
    for other in others:
        total = total + other.astype(F32)
    return total.astype(BF)


def add_pair(a, b):
    return add_all(a, b)


def halve(part, mask):
    rows = part.shape[0] // 2
    return add_pair(part[:rows], swap(part[rows:], "tile", mask))


def shards(
    feats, cotangent, w_reduce, w_group, w_expand, scale1, shift1, scale2, shift2,
    scale3, shift3, tile_count, joined,
):
    devices = lax.axis_size("tile")
    slides = lax.axis_size("slide")
    per = MID // devices
    x, g = feats[0], cotangent[0]
    s1, b1, s2, b2 = (v.reshape(1, MID) for v in (scale1, shift1, scale2, shift2))
    s3, b3 = (v.reshape(1, CIN) for v in (scale3, shift3))

    to_core, to_other, meta = call(
        edge_kernel, "edges",
        [shape((PAY, CIN), BF), shape((PAY, CIN), BF), shape((META,), jnp.int32)],
        (), (0, 1, 2, 3), 4,
        [pltpu.SMEM(tile_count.shape, jnp.int32), pltpu.SMEM(joined.shape, jnp.int32),
         pltpu.VMEM((SLOTS, CIN, PIX), BF), pltpu.VMEM((SLOTS, CIN, PIX), BF), pltpu.SemaphoreType.DMA((4,))],
        (2,),
    )(tile_count, joined, x, g)
    hops = [(i, i + 1) for i in range(1, devices - 1, 2)]
    from_other = lax.ppermute(to_other, "tile", hops + [(b, a) for a, b in hops])
    from_core = swap(to_core, "tile", 1)

    hid, slope_a, dense, denset, wet = call(
        prep_kernel, "prep",
        [shape((SLOTS, MID, PIX), BF), shape((SLOTS, MID, PIX), F32), shape((2, HALF, KDIM), BF),
         shape((2, HALF, KDIM), BF), shape((CIN, MID), BF)],
        (0,), (), 7,
    )(meta, x, w_reduce, w_expand, w_group.T, s1, b1)

    lanes = SLOTS * PIX
    act, back, errc, slope_b, hid, edge, hid_e, slope_e, e_send, e_keep = call(
        functools.partial(forward_kernel, devices), "forward",
        [shape((SLOTS, CIN, PIX), BF), shape((SLOTS, CIN, PIX), F32), shape((CIN, lanes), BF),
         shape((MID, lanes), F32), shape((SLOTS + 2, MID, PIX), BF), shape((CIN, PIX), BF),
         shape((MID, PIX), BF), shape((MID, PIX), F32), shape((devices // 2, 8 * per, PIX), BF), shape((devices // 2, 8 * per, PIX), BF)],
        (0,), (), 15,
        [pltpu.VMEM((2, KDIM, lanes), BF), pltpu.VMEM((2, KDIM, PIX), BF), pltpu.VMEM((MID, lanes), BF)],
    )(meta, from_core, from_other, hid, w_reduce, s1, b1, dense, s2, b2, wet, s3, b3, x, g)

    e_core = swap(e_send, "tile", 1)
    (errb,) = call(
        pull_kernel, "pull", [shape((SLOTS + 2, MID, PIX), BF)], (), (), 11,
    )(from_core, from_other, hid_e, slope_e, wet, s3, b3, edge, w_expand, errc, slope_b)
    e_part = add_pair(e_keep, e_core)
    errb, e_part = lax.optimization_barrier((errb, e_part))
    e_part = halve(e_part, 2)

    piece = [shape((devices // 8, 9 * per + 8, PIX), BF)] * 8
    erra, *pieces = call(
        functools.partial(backward_kernel, devices), "backward", [shape((SLOTS, MID, PIX), BF)] + piece,
        (0,), (), 7,
        [pltpu.VMEM((2, KDIM, lanes), BF), pltpu.VMEM((MID, lanes), BF), pltpu.VMEM((MID, HALF), BF),
         pltpu.VMEM((HALF, KDIM), BF)],
    )(meta, errb, hid, slope_a, denset, x, tap_places())
    (grad_in, out) = call(
        grad_kernel, "grads", [shape((SLOTS, CIN, PIX), BF), shape((SLOTS, CIN, PIX), BF)], (), (), 4,
    )(w_reduce, erra, back, act)

    r_core = [swap(value, "tile", 1) for value in pieces[:4]]
    *r_core, e_part = lax.optimization_barrier((*r_core, e_part))
    r_parts = [add_pair(a, b) for a, b in zip(pieces[4:], r_core)]
    tall, half = r_parts[1].shape[1], e_part.shape[0] // 2
    r_parts[1] = jnp.concatenate([r_parts[1], e_part[half:]], axis=1)
    r_parts = [r_parts[0]] + [cross(r_parts[k], devices, slides, 2 * (k // 2 + 2 * (k % 2)), 0) for k in (1, 2, 3)]
    e_part = add_pair(e_part[:half], r_parts[1][:, tall:])
    r_parts[1] = r_parts[1][:, :tall]
    mask = 8
    while mask < devices:
        e_part = halve(e_part, mask)
        mask *= 2
    r_part = add_all(*r_parts)
    mask = 8
    while 2 * mask < devices:
        r_part = halve(r_part, mask)
        mask *= 2
    mine, theirs = r_part[0], r_part[1]
    near = mine.shape[0]
    both = cross(jnp.concatenate([mine, e_part[0]], axis=0), devices, slides, 0, 1)
    e_other = both[near:]
    finals = [
        mine,
        both[:near],
        cross(theirs, devices, slides, devices // 2, 0),
        cross(theirs, devices, slides, devices // 2, 1),
    ]
    if slides > 2:
        e_part, e_other = add_pair(e_part, e_other[None]), jnp.zeros_like(e_other)
        total = add_all(*finals)
        mask = 2
        while mask < slides:
            e_part = add_pair(e_part, swap(e_part, "slide", mask))
            total = add_pair(total, swap(total, "slide", mask))
            mask *= 2
        finals = [total] + [jnp.zeros_like(total)] * 3
    norm = 1.0 / math.sqrt(slides * LIVE_DEV * devices * PIX)
    grad_reduce, grad_group, grad_expand = call(
        functools.partial(finish_kernel, norm), "finish",
        [shape((per, CIN), F32), shape((per, TAPS * GW), F32), shape((per, CIN), F32)], (), (), 6,
    )(e_part[0], e_other, *finals)
    return (out[None], grad_in[None], grad_reduce, grad_group, grad_expand)


def solution(mesh):
    tiles = P("slide", "tile", None, None)
    in_specs = (tiles, tiles) + (P(),) * 9 + (P("slide", None), P("slide", None))
    out_specs = (tiles, tiles, P("tile", None), P("tile", None), P("tile", None))
    return jax.shard_map(shards, mesh=mesh, in_specs=in_specs, out_specs=out_specs, check_vma=False)
```

```python
import functools
import math

import jax
import jax.numpy as jnp
import numpy as np
from jax import lax
from jax.experimental import pallas as pl
from jax.experimental.pallas import tpu as pltpu
from jax.sharding import PartitionSpec as P

CIN = 1024
MID = 512
GW = 16
TH = 16
TW = 8
PIX = 128
SLOTS = 4
HALF = 256
TAPS = 9
KDIM = TAPS * HALF
PAY = 48
LIVE_DEV = 2
BF = jnp.bfloat16
F32 = jnp.float32

HELD, L_IDX, R_IDX, META = 0, 1, 6, 16
EDGE, ZERO = SLOTS, SLOTS + 1


def nt_dot(a, b):
    return lax.dot_general(a, b, (((1,), (1,)), ((), ())), preferred_element_type=F32)


def tn_dot(a, b):
    return lax.dot_general(a, b, (((0,), (0,)), ((), ())), preferred_element_type=F32)


def nn_dot(a, b):
    return lax.dot_general(a, b, (((1,), (0,)), ((), ())), preferred_element_type=F32)


def sigmoid(v):
    return 0.5 * jnp.tanh(0.5 * v) + 0.5


def column(row_ref):
    row = row_ref[...]
    return jnp.transpose(jnp.broadcast_to(row, (PIX, row.shape[1])))


def wide(col, lanes):
    return jnp.concatenate([col] * (lanes // PIX), axis=1)


def edge_select(rows, lane_of):
    row = lax.broadcasted_iota(jnp.int32, (rows, PIX), 0)
    lane = lax.broadcasted_iota(jnp.int32, (rows, PIX), 1)
    return (lane == lane_of(row)).astype(F32).astype(BF)


def x_lane(first):
    return lambda row: (row % TH) * TW + row // TH + first


def g_lane(col):
    return lambda row: row * TW + col


def edge_kernel(
    count_hbm, joined_hbm, x_any, g_any, core_ref, other_ref, meta_ref,
    count_ref, joined_ref, xbuf, gbuf, sems,
):
    me = lax.axis_index("tile")
    tables = [
        pltpu.make_async_copy(count_hbm, count_ref, sems.at[2]),
        pltpu.make_async_copy(joined_hbm, joined_ref, sems.at[3]),
    ]
    loads = [pltpu.make_async_copy(x_any, xbuf, sems.at[0]), pltpu.make_async_copy(g_any, gbuf, sems.at[1])]
    for copy in tables + loads:
        copy.start()
    for copy in tables:
        copy.wait()
    devices = count_ref.shape[1]
    links = joined_ref.shape[1]
    start = jnp.int32(0)
    held = jnp.int32(0)
    for e in range(devices):
        start = start + jnp.where(e < me, count_ref[0, e], 0)
        held = held + jnp.where(e == me, count_ref[0, e], 0)
    last = held - 1
    def joined_to(at, neighbour):
        inside = jnp.logical_and(at >= 0, at < links)
        on = joined_ref[0, jnp.clip(at, 0, links - 1)] != 0
        return jnp.where(jnp.logical_and(inside, on), neighbour, ZERO).astype(jnp.int32)

    meta_ref[HELD] = held
    for i in range(SLOTS):
        left = joined_to(start + i - 1, EDGE if i == 0 else i - 1)
        right = joined_to(start + i, jnp.where(i >= last, EDGE, i + 1))
        meta_ref[L_IDX + i] = jnp.where(i < held, left, ZERO).astype(jnp.int32)
        meta_ref[R_IDX + i] = jnp.where(i < held, right, ZERO).astype(jnp.int32)
    meta_ref[L_IDX + EDGE] = joined_to(start + last, last)
    meta_ref[R_IDX + EDGE] = joined_to(start - 1, 0)

    for copy in loads:
        copy.wait()
    even = me % 2 == 0

    def payload(slot, x_first, g_col):
        return (
            nt_dot(edge_select(2 * TH, x_lane(x_first)), xbuf[slot]).astype(BF),
            nt_dot(edge_select(TH, g_lane(g_col)), gbuf[slot]).astype(BF),
        )

    left_x, left_g = payload(0, 0, 0)
    right_x, right_g = payload(last, TW - 2, TW - 1)

    @pl.when(even)
    def _():
        core_ref[: 2 * TH] = right_x
        core_ref[2 * TH :] = right_g
        other_ref[: 2 * TH] = left_x
        other_ref[2 * TH :] = left_g

    @pl.when(jnp.logical_not(even))
    def _():
        core_ref[: 2 * TH] = left_x
        core_ref[2 * TH :] = left_g
        other_ref[: 2 * TH] = right_x
        other_ref[2 * TH :] = right_g


def prep_kernel(
    x_ref, wr_ref, we_ref, wg_ref, s1_ref, b1_ref, s2_ref, b2_ref, s3_ref, b3_ref,
    hid_ref, slope_ref, dense_ref, denset_ref, wet_ref, mid_ref, end_ref, part_ref, win_ref,
):
    scale = column(s1_ref)
    shift = column(b1_ref)
    mid_ref[0] = scale
    mid_ref[1] = shift
    mid_ref[2] = column(s2_ref)
    mid_ref[3] = column(b2_ref)
    end_ref[0] = column(s3_ref)
    end_ref[1] = column(b3_ref)
    for half in range(SLOTS // 2):
        tiles = jnp.concatenate([x_ref[2 * half], x_ref[2 * half + 1]], axis=1)
        reduced = nn_dot(wr_ref[...], tiles)
        for k in range(2):
            i = 2 * half + k
            pre = reduced[:, k * PIX : (k + 1) * PIX] * scale + shift
            sig = sigmoid(pre)
            act = pre * sig
            hid_ref[i] = act.astype(BF)
            slope_ref[i] = (sig + act * (1.0 - sig)) * scale
    tap_row = lax.broadcasted_iota(jnp.int32, (TAPS * GW, KDIM), 0)
    lane = lax.broadcasted_iota(jnp.int32, (TAPS * GW, KDIM), 1)
    block = lane // HALF
    tap = 3 * (block % 3) + jnp.where(block < 3, 1, jnp.where(block < 6, 0, 2))
    pick = (tap_row == tap * GW + lane % GW).astype(F32).astype(BF)
    spread = tn_dot(wg_ref[...], pick)
    row = lax.broadcasted_iota(jnp.int32, (MID, KDIM), 0)
    col = lax.broadcasted_iota(jnp.int32, (MID, KDIM), 1)
    keep = (row % HALF) // GW == (col % HALF) // GW
    dense_ref[...] = jnp.where(keep, spread, 0.0).astype(BF).reshape(2, HALF, KDIM)
    row_t = lax.broadcasted_iota(jnp.int32, (HALF, MID), 0)
    col_t = lax.broadcasted_iota(jnp.int32, (HALF, MID), 1)
    keep_t = row_t // GW == (col_t % HALF) // GW
    prow = lax.broadcasted_iota(jnp.int32, (HALF, TAPS * GW), 0)
    pcol = lax.broadcasted_iota(jnp.int32, (HALF, TAPS * GW), 1)
    for k in range(TAPS):
        pick_t = (pcol == k * GW + prow % GW).astype(F32).astype(BF)
        spread_t = jnp.where(keep_t, nn_dot(pick_t, wg_ref[...]), 0.0).astype(BF)
        for b in range(2):
            denset_ref[b, :, k * HALF : (k + 1) * HALF] = spread_t[:, b * HALF : (b + 1) * HALF]
    wet_ref[...] = jnp.transpose(we_ref[...])
    lane = lax.broadcasted_iota(jnp.int32, (HALF, PIX), 1)
    for i in range(SLOTS):
        for b in range(2):
            shifts = row_shifts(hid_ref[i, b * HALF : (b + 1) * HALF, :], lane >= TW, lane < PIX - TW)
            for u, shifted in enumerate(shifts):
                win_ref[b, u * HALF : (u + 1) * HALF, i * PIX : (i + 1) * PIX] = shifted
    for b in range(2):
        part_ref[b * HALF : (b + 1) * HALF, :] = nn_dot(dense_ref[b, :, :MIDDLE], win_ref[b])


def silu_slope(v):
    sig = sigmoid(v)
    act = v * sig
    return act, sig + act * (1.0 - sig)


MIDDLE = 3 * HALF


def forward_place(u, v):
    return (1, 0, 2)[v] * 3 + u


def side_place(u, v):
    return None if v == 1 else forward_place(u, v) - 3


def transposed_place(u, v):
    return TAPS - 1 - (3 * u + v)


def row_shifts(base, has_above, has_below):
    zero = jnp.zeros((), BF)
    return (
        jnp.where(has_above, pltpu.roll(base, TW, 1), zero),
        base,
        jnp.where(has_below, pltpu.roll(base, PIX - TW, 1), zero),
    )


def build_windows(field_ref, win_ref, meta_ref, tiles, first, place):
    lane = lax.broadcasted_iota(jnp.int32, (HALF, PIX), 1)
    col = lane % TW
    first_col = col == 0
    last_col = col == TW - 1
    has_above = lane >= TW
    has_below = lane < PIX - TW
    for i in tiles:
        left_at = meta_ref[L_IDX + i]
        right_at = meta_ref[R_IDX + i]
        lanes = pl.ds((i - first) * PIX, PIX)
        for b in range(2):
            rows = pl.ds(b * HALF, HALF)
            own = field_ref[i, rows, :]
            left = field_ref[left_at, rows, :]
            right = field_ref[right_at, rows, :]
            west = jnp.where(first_col, pltpu.roll(left, PIX - TW + 1, 1), pltpu.roll(own, 1, 1))
            east = jnp.where(last_col, pltpu.roll(right, TW - 1, 1), pltpu.roll(own, PIX - 1, 1))
            for v, base in enumerate((west, own, east)):
                if place(0, v) is None:
                    continue
                for u, shifted in enumerate(row_shifts(base, has_above, has_below)):
                    win_ref[b, pl.ds(place(u, v) * HALF, HALF), lanes] = shifted


CHUNKS = ((0, 2), (2, 2))


def forward_kernel(
    devices, meta_ref, core_ref, other_ref, hid_in, wr_ref, dense_ref, wet_ref, mid_ref, end_ref, part_ref, x_ref, g_ref,
    out_ref, back_ref, errc_ref, slopeb_ref, hid_ref, edge_ref, hide_ref, slopee_ref, send_ref, keep_ref,
    win_ref, wine_ref, hidb_ref,
):
    me = lax.axis_index("tile")
    held = meta_ref[HELD]
    odd = me % 2
    core_first = jnp.where(odd == 0, 0, TW - 2)
    other_first = jnp.where(odd == 0, TW - 2, 0)
    edge_x = (
        tn_dot(core_ref[: 2 * TH, :], edge_select(2 * TH, x_lane(core_first)))
        + tn_dot(other_ref[: 2 * TH, :], edge_select(2 * TH, x_lane(other_first)))
    ).astype(BF)
    edge_ref[...] = edge_x
    for i in range(SLOTS):
        hid_ref[i] = hid_in[i]
    pre = nn_dot(wr_ref[...], edge_x) * mid_ref[0] + mid_ref[1]
    hid_ref[EDGE] = (pre * sigmoid(pre)).astype(BF)
    hid_ref[ZERO] = jnp.zeros((MID, PIX), BF)

    build_windows(hid_ref, wine_ref, meta_ref, (EDGE,), EDGE, forward_place)
    for b in range(2):
        rows = slice(b * HALF, (b + 1) * HALF)
        act, slope = silu_slope(nn_dot(dense_ref[b], wine_ref[b]) * mid_ref[2, rows, :] + mid_ref[3, rows, :])
        hide_ref[rows, :] = act.astype(BF)
        slopee_ref[rows, :] = slope * mid_ref[2, rows, :]

    for first, count in CHUNKS:
        build_windows(hid_ref, win_ref, meta_ref, range(first, first + count), 0, side_place)
        lanes = slice(first * PIX, (first + count) * PIX)
        for b in range(2):
            rows = slice(b * HALF, (b + 1) * HALF)
            conv = nn_dot(dense_ref[b, :, MIDDLE:], win_ref[b, :, lanes]) + part_ref[rows, lanes]
            for k in range(count):
                at = slice((first + k) * PIX, (first + k + 1) * PIX)
                act, slope = silu_slope(conv[:, k * PIX : (k + 1) * PIX] * mid_ref[2, rows, :] + mid_ref[3, rows, :])
                hidb_ref[rows, at] = act.astype(BF)
                slopeb_ref[rows, at] = slope * mid_ref[2, rows, :]
        grown = nn_dot(wet_ref[...], hidb_ref[:, lanes])
        for k in range(count):
            i = first + k
            act, slope = silu_slope(
                grown[:, k * PIX : (k + 1) * PIX] * end_ref[0] + end_ref[1] + x_ref[i].astype(F32)
            )
            live = jnp.where(i < held, 1.0, 0.0).astype(F32)
            back = g_ref[i].astype(F32) * slope * live
            out_ref[i] = (act * live).astype(BF)
            back_ref[i] = back
            errc_ref[:, i * PIX : (i + 1) * PIX] = (back * end_ref[0]).astype(BF)

    own = SLOTS * PIX
    for ref, flip in ((send_ref, 1), (keep_ref, 0)):
        rows = jnp.concatenate([hidb_ref[at, :own] for at in row_blocks(devices, me, flip)], axis=0)
        part = nt_dot(rows, errc_ref[:, :own]).astype(BF)
        per = MID // devices
        for j in range(devices // 2):
            for c in range(CIN // PIX):
                ref[j, c * per : (c + 1) * per, :] = part[j * per : (j + 1) * per, c * PIX : (c + 1) * PIX]


def row_blocks(devices, me, flip):
    per = MID // devices
    bits = (devices // 2).bit_length() - 1
    blocks = []
    for j in range(devices // 2):
        distance = flip
        for bit in range(bits):
            distance |= ((j >> (bits - 1 - bit)) & 1) << (bit + 1)
        at = pl.multiple_of((me ^ distance) * per, per)
        blocks.append(pl.ds(at, per))
    return blocks


def pull_kernel(
    core_ref, other_ref, hide_ref, slopee_ref, wet_ref, end_ref,
    edge_ref, we_ref, errc_ref, slopeb_ref, errb_ref,
):
    odd = lax.axis_index("tile") % 2
    core_g = jnp.where(odd == 0, 0, TW - 1)
    other_g = jnp.where(odd == 0, TW - 1, 0)
    edge_g = (
        tn_dot(core_ref[2 * TH :, :], edge_select(TH, g_lane(core_g)))
        + tn_dot(other_ref[2 * TH :, :], edge_select(TH, g_lane(other_g)))
    )
    for first, count in CHUNKS:
        lanes = slice(first * PIX, (first + count) * PIX)
        pulled = nn_dot(we_ref[...], errc_ref[:, lanes])
        errb = (pulled * slopeb_ref[:, lanes]).astype(BF)
        for k in range(count):
            errb_ref[first + k] = errb[:, k * PIX : (k + 1) * PIX]
    grown = nn_dot(wet_ref[...], hide_ref[...])
    _, slope = silu_slope(grown * end_ref[0] + end_ref[1] + edge_ref[...].astype(F32))
    errc = (edge_g * slope * end_ref[0]).astype(BF)
    errb_ref[EDGE] = (nn_dot(we_ref[...], errc) * slopee_ref[...]).astype(BF)
    errb_ref[ZERO] = jnp.zeros((MID, PIX), BF)


def backward_kernel(
    devices, meta_ref, errb_ref, hid_ref, slope_ref, denset_ref, x_ref, place_ref,
    erra_ref, *rest,
):
    send_refs, keep_refs = rest[:4], rest[4:8]
    win_ref, flat_ref, groups_ref, kept_ref = rest[8:]
    me = lax.axis_index("tile")
    held = meta_ref[HELD]
    for first, count in CHUNKS:
        build_windows(errb_ref, win_ref, meta_ref, range(first, first + count), 0, transposed_place)
        lanes = slice(first * PIX, (first + count) * PIX)
        for b in range(2):
            conv = nn_dot(denset_ref[b], win_ref[b, :, lanes])
            rows = slice(b * HALF, (b + 1) * HALF)
            for k in range(count):
                i = first + k
                live = jnp.where(i < held, 1.0, 0.0).astype(F32)
                err = (conv[:, k * PIX : (k + 1) * PIX] * slope_ref[i, rows, :] * live).astype(BF)
                flat_ref[rows, i * PIX : (i + 1) * PIX] = err
                erra_ref[i, rows, :] = err
    row = lax.broadcasted_iota(jnp.int32, (HALF, HALF), 0)
    col = lax.broadcasted_iota(jnp.int32, (HALF, HALF), 1)
    same = row // GW == col // GW
    for b in range(2):
        rows = slice(b * HALF, (b + 1) * HALF)
        hid = jnp.transpose(jnp.concatenate([hid_ref[i, rows, :] for i in range(SLOTS)], axis=1))
        for k in range(TAPS):
            full = nn_dot(win_ref[b, k * HALF : (k + 1) * HALF, :], hid)
            kept_ref[:, k * HALF : (k + 1) * HALF] = jnp.where(same, full, 0.0).astype(BF)
        groups_ref[rows, :] = nn_dot(kept_ref[...], place_ref[...]).astype(BF)
    tiles = jnp.concatenate([x_ref[i] for i in range(SLOTS)], axis=1)
    per = MID // devices
    inner = devices // 8
    lane = lax.broadcasted_iota(jnp.int32, (HALF, PIX), 1)
    row = lax.broadcasted_iota(jnp.int32, (HALF, PIX), 0)
    own_lanes = lane // GW == row % 8
    lane = lax.broadcasted_iota(jnp.int32, (PIX, PIX), 1)
    row = lax.broadcasted_iota(jnp.int32, (PIX, PIX), 0)
    repeat = (lane % GW == row).astype(F32).astype(BF)
    pack = lax.broadcasted_iota(jnp.int32, (4 * devices, HALF), 0)
    row = lax.broadcasted_iota(jnp.int32, (4 * devices, HALF), 1)
    gather = jnp.logical_and(pack // 8 == row // per, pack % 8 == (row % per) // 8).astype(F32).astype(BF)
    for refs, flip in ((send_refs, 1), (keep_refs, 0)):
        blocks = row_blocks(devices, me, flip)
        rows = jnp.concatenate([flat_ref[at, :] for at in blocks], axis=0)
        group_rows = jnp.concatenate([groups_ref[at, :] for at in blocks], axis=0)
        part = nt_dot(rows, tiles).astype(BF)
        tail = jnp.where(own_lanes, nn_dot(group_rows[:, PIX:], repeat), 0.0).astype(BF)
        tail = nn_dot(gather, tail).astype(BF)
        for j in range(devices // 2):
            ref, i = refs[j // inner], j % inner
            at = slice(j * per, (j + 1) * per)
            for c in range(CIN // PIX):
                ref[i, c * per : (c + 1) * per, :] = part[at, c * PIX : (c + 1) * PIX]
            ref[i, 8 * per : 9 * per, :] = group_rows[at, :PIX]
            ref[i, 9 * per :, :] = tail[8 * j : 8 * j + 8]


def grad_kernel(wr_ref, erra_ref, back_ref, act_ref, grad_ref, out_ref):
    out_ref[...] = act_ref[...]
    for half in range(SLOTS // 2):
        err = jnp.concatenate([erra_ref[2 * half], erra_ref[2 * half + 1]], axis=1)
        pulled = tn_dot(wr_ref[...], err)
        for k in range(2):
            i = 2 * half + k
            grad_ref[i] = (pulled[:, k * PIX : (k + 1) * PIX] + back_ref[i]).astype(BF)


def finish_kernel(norm, ea_ref, eb_ref, *refs):
    parts, (reduce_ref, group_ref, expand_ref) = refs[:4], refs[4:]
    expand = (ea_ref[...].astype(F32) + eb_ref[...].astype(F32)) * norm
    total = sum(part[...].astype(F32) for part in parts) * norm
    per = reduce_ref.shape[0]
    for c in range(CIN // PIX):
        reduce_ref[:, c * PIX : (c + 1) * PIX] = total[c * per : (c + 1) * per]
        expand_ref[:, c * PIX : (c + 1) * PIX] = expand[c * per : (c + 1) * per]
    group_ref[:, :PIX] = total[8 * per : 9 * per]
    tail = jnp.concatenate(
        [jnp.broadcast_to(total[9 * per + k : 9 * per + k + 1], (8, PIX)) for k in range(per // 8)], axis=0
    )
    lane = lax.broadcasted_iota(jnp.int32, (per, PIX), 1)
    row = lax.broadcasted_iota(jnp.int32, (per, PIX), 0)
    tail = jnp.where(lane // GW == row % 8, tail, 0.0)
    for shift in (64, 32, 16):
        tail = tail + pltpu.roll(tail, shift, 1)
    group_ref[:, PIX:] = tail[:, : TAPS * GW - PIX]


LIMITS = {"edges": 56, "prep": 20, "forward": 28, "pull": 12, "backward": 18, "grads": 9, "finish": 2}
WORK = {"edges": 2, "prep": 3, "forward": 7, "pull": 2, "backward": 5, "grads": 2, "finish": 1}


def call(body, name, out_shape, in_smem, in_any, n_in, scratch=(), out_smem=()):
    vmem = pl.BlockSpec(memory_space=pltpu.VMEM)
    smem = pl.BlockSpec(memory_space=pltpu.SMEM)
    anys = pl.BlockSpec(memory_space=pltpu.HBM)
    return pl.pallas_call(
        body,
        name=name,
        out_shape=out_shape,
        in_specs=[smem if i in in_smem else anys if i in in_any else vmem for i in range(n_in)],
        out_specs=[smem if i in out_smem else vmem for i in range(len(out_shape))],
        scratch_shapes=list(scratch),
        compiler_params=pltpu.CompilerParams(vmem_limit_bytes=LIMITS[name] * 1024 * 1024),
        cost_estimate=pl.CostEstimate(flops=int(WORK[name] * 1.1e9), bytes_accessed=1 << 20, transcendentals=0),
    )


def shape(dims, dtype):
    return jax.ShapeDtypeStruct(dims, dtype)


def swap(value, axis, mask):
    size = lax.axis_size(axis)
    return lax.ppermute(value, axis, [(i, i ^ mask) for i in range(size)])


def tap_places():
    row = np.arange(KDIM)
    place = np.zeros((KDIM, HALF), np.float32)
    place[row, row // HALF * GW + row % GW] = 1.0
    return jnp.asarray(place, BF)


def cross(value, devices, slides, tile_mask, slide_mask):
    pairs = [
        (t * slides + k, (t ^ tile_mask) * slides + (k ^ slide_mask))
        for t in range(devices)
        for k in range(slides)
    ]
    return lax.ppermute(value, ("tile", "slide"), pairs)


def spread(part, devices, slides):
    rows = part.shape[0] // 4
    return [part[:rows]] + [
        cross(part[k * rows : (k + 1) * rows], devices, slides, 2 * (k // 2 + 2 * (k % 2)), 0) for k in (1, 2, 3)
    ]


def add_all(first, *others):
    total = first.astype(F32)
    for other in others:
        total = total + other.astype(F32)
    return total.astype(BF)


def add_pair(a, b):
    return add_all(a, b)


def halve(part, mask):
    rows = part.shape[0] // 2
    return add_pair(part[:rows], swap(part[rows:], "tile", mask))


def shards(
    feats, cotangent, w_reduce, w_group, w_expand, scale1, shift1, scale2, shift2,
    scale3, shift3, tile_count, joined,
):
    devices = lax.axis_size("tile")
    slides = lax.axis_size("slide")
    per = MID // devices
    x, g = feats[0], cotangent[0]
    s1, b1, s2, b2 = (v.reshape(1, MID) for v in (scale1, shift1, scale2, shift2))
    s3, b3 = (v.reshape(1, CIN) for v in (scale3, shift3))

    to_core, to_other, meta = call(
        edge_kernel, "edges",
        [shape((PAY, CIN), BF), shape((PAY, CIN), BF), shape((META,), jnp.int32)],
        (), (0, 1, 2, 3), 4,
        [pltpu.SMEM(tile_count.shape, jnp.int32), pltpu.SMEM(joined.shape, jnp.int32),
         pltpu.VMEM((SLOTS, CIN, PIX), BF), pltpu.VMEM((SLOTS, CIN, PIX), BF), pltpu.SemaphoreType.DMA((4,))],
        (2,),
    )(tile_count, joined, x, g)
    hops = [(i, i + 1) for i in range(1, devices - 1, 2)]
    from_other = lax.ppermute(to_other, "tile", hops + [(b, a) for a, b in hops])
    from_core = swap(to_core, "tile", 1)

    hid, slope_a, dense, denset, wet, mid, end, part = call(
        prep_kernel, "prep",
        [shape((SLOTS, MID, PIX), BF), shape((SLOTS, MID, PIX), F32), shape((2, HALF, KDIM), BF),
         shape((2, HALF, KDIM), BF), shape((CIN, MID), BF), shape((4, MID, PIX), F32), shape((2, CIN, PIX), F32),
         shape((MID, SLOTS * PIX), F32)],
        (), (), 10, [pltpu.VMEM((2, MIDDLE, SLOTS * PIX), BF)],
    )(x, w_reduce, w_expand, w_group.T, s1, b1, s2, b2, s3, b3)

    lanes = SLOTS * PIX
    act, back, errc, slope_b, hid, edge, hid_e, slope_e, e_send, e_keep = call(
        functools.partial(forward_kernel, devices), "forward",
        [shape((SLOTS, CIN, PIX), BF), shape((SLOTS, CIN, PIX), F32), shape((CIN, lanes), BF),
         shape((MID, lanes), F32), shape((SLOTS + 2, MID, PIX), BF), shape((CIN, PIX), BF),
         shape((MID, PIX), BF), shape((MID, PIX), F32), shape((devices // 2, 8 * per, PIX), BF), shape((devices // 2, 8 * per, PIX), BF)],
        (0,), (), 12,
        [pltpu.VMEM((2, KDIM - MIDDLE, lanes), BF), pltpu.VMEM((2, KDIM, PIX), BF), pltpu.VMEM((MID, lanes), BF)],
    )(meta, from_core, from_other, hid, w_reduce, dense, wet, mid, end, part, x, g)

    e_core = swap(e_send, "tile", 1)
    (errb,) = call(
        pull_kernel, "pull", [shape((SLOTS + 2, MID, PIX), BF)], (), (), 10,
    )(from_core, from_other, hid_e, slope_e, wet, end, edge, w_expand, errc, slope_b)
    e_part = add_pair(e_keep, e_core)
    errb, e_part = lax.optimization_barrier((errb, e_part))
    e_part = halve(e_part, 2)

    piece = [shape((devices // 8, 9 * per + 8, PIX), BF)] * 8
    erra, *pieces = call(
        functools.partial(backward_kernel, devices), "backward", [shape((SLOTS, MID, PIX), BF)] + piece,
        (0,), (), 7,
        [pltpu.VMEM((2, KDIM, lanes), BF), pltpu.VMEM((MID, lanes), BF), pltpu.VMEM((MID, HALF), BF),
         pltpu.VMEM((HALF, KDIM), BF)],
    )(meta, errb, hid, slope_a, denset, x, tap_places())
    (grad_in, out) = call(
        grad_kernel, "grads", [shape((SLOTS, CIN, PIX), BF), shape((SLOTS, CIN, PIX), BF)], (), (), 4,
    )(w_reduce, erra, back, act)

    r_core = [swap(value, "tile", 1) for value in pieces[:4]]
    *r_core, e_part = lax.optimization_barrier((*r_core, e_part))
    r_parts = [add_pair(a, b) for a, b in zip(pieces[4:], r_core)]
    tall, half = r_parts[1].shape[1], e_part.shape[0] // 2
    r_parts[1] = jnp.concatenate([r_parts[1], e_part[half:]], axis=1)
    r_parts = [r_parts[0]] + [cross(r_parts[k], devices, slides, 2 * (k // 2 + 2 * (k % 2)), 0) for k in (1, 2, 3)]
    e_part = add_pair(e_part[:half], r_parts[1][:, tall:])
    r_parts[1] = r_parts[1][:, :tall]
    mask = 8
    while mask < devices:
        e_part = halve(e_part, mask)
        mask *= 2
    r_part = add_all(*r_parts)
    mask = 8
    while 2 * mask < devices:
        r_part = halve(r_part, mask)
        mask *= 2
    mine, theirs = r_part[0], r_part[1]
    near = mine.shape[0]
    both = cross(jnp.concatenate([mine, e_part[0]], axis=0), devices, slides, 0, 1)
    e_other = both[near:]
    finals = [
        mine,
        both[:near],
        cross(theirs, devices, slides, devices // 2, 0),
        cross(theirs, devices, slides, devices // 2, 1),
    ]
    if slides > 2:
        e_part, e_other = add_pair(e_part, e_other[None]), jnp.zeros_like(e_other)
        total = add_all(*finals)
        mask = 2
        while mask < slides:
            e_part = add_pair(e_part, swap(e_part, "slide", mask))
            total = add_pair(total, swap(total, "slide", mask))
            mask *= 2
        finals = [total] + [jnp.zeros_like(total)] * 3
    norm = 1.0 / math.sqrt(slides * LIVE_DEV * devices * PIX)
    grad_reduce, grad_group, grad_expand = call(
        functools.partial(finish_kernel, norm), "finish",
        [shape((per, CIN), F32), shape((per, TAPS * GW), F32), shape((per, CIN), F32)], (), (), 6,
    )(e_part[0], e_other, *finals)
    return (out[None], grad_in[None], grad_reduce, grad_group, grad_expand)


def solution(mesh):
    tiles = P("slide", "tile", None, None)
    in_specs = (tiles, tiles) + (P(),) * 9 + (P("slide", None), P("slide", None))
    out_specs = (tiles, tiles, P("tile", None), P("tile", None), P("tile", None))
    return jax.shard_map(shards, mesh=mesh, in_specs=in_specs, out_specs=out_specs, check_vma=False)
```

```python
import functools
import math

import jax
import jax.numpy as jnp
import numpy as np
from jax import lax
from jax.experimental import pallas as pl
from jax.experimental.pallas import tpu as pltpu
from jax.sharding import PartitionSpec as P

CIN = 1024
MID = 512
GW = 16
TH = 16
TW = 8
PIX = 128
SLOTS = 4
HALF = 256
TAPS = 9
KDIM = TAPS * HALF
PAY = 48
LIVE_DEV = 2
BF = jnp.bfloat16
F32 = jnp.float32

HELD, L_IDX, R_IDX, META = 0, 1, 6, 16
EDGE, ZERO = SLOTS, SLOTS + 1


def nt_dot(a, b):
    return lax.dot_general(a, b, (((1,), (1,)), ((), ())), preferred_element_type=F32)


def tn_dot(a, b):
    return lax.dot_general(a, b, (((0,), (0,)), ((), ())), preferred_element_type=F32)


def nn_dot(a, b):
    return lax.dot_general(a, b, (((1,), (0,)), ((), ())), preferred_element_type=F32)


def sigmoid(v):
    return 0.5 * jnp.tanh(0.5 * v) + 0.5


def column(row_ref):
    row = row_ref[...]
    return jnp.transpose(jnp.broadcast_to(row, (PIX, row.shape[1])))


def wide(col, lanes):
    return jnp.concatenate([col] * (lanes // PIX), axis=1)


def edge_select(rows, lane_of):
    row = lax.broadcasted_iota(jnp.int32, (rows, PIX), 0)
    lane = lax.broadcasted_iota(jnp.int32, (rows, PIX), 1)
    return (lane == lane_of(row)).astype(F32).astype(BF)


def x_lane(first):
    return lambda row: (row % TH) * TW + row // TH + first


def g_lane(col):
    return lambda row: row * TW + col


def edge_kernel(
    count_hbm, joined_hbm, x_any, g_any, core_ref, other_ref, meta_ref,
    count_ref, joined_ref, xbuf, gbuf, sems,
):
    me = lax.axis_index("tile")
    tables = [
        pltpu.make_async_copy(count_hbm, count_ref, sems.at[2]),
        pltpu.make_async_copy(joined_hbm, joined_ref, sems.at[3]),
    ]
    firsts = [
        pltpu.make_async_copy(x_any.at[0], xbuf.at[0], sems.at[0]),
        pltpu.make_async_copy(g_any.at[0], gbuf.at[0], sems.at[1]),
    ]
    loads = [
        pltpu.make_async_copy(x_any.at[1:], xbuf.at[1:], sems.at[4]),
        pltpu.make_async_copy(g_any.at[1:], gbuf.at[1:], sems.at[5]),
    ]
    for copy in tables + firsts + loads:
        copy.start()
    for copy in tables:
        copy.wait()
    devices = count_ref.shape[1]
    links = joined_ref.shape[1]
    start = jnp.int32(0)
    held = jnp.int32(0)
    for e in range(devices):
        start = start + jnp.where(e < me, count_ref[0, e], 0)
        held = held + jnp.where(e == me, count_ref[0, e], 0)
    last = held - 1
    def joined_to(at, neighbour):
        inside = jnp.logical_and(at >= 0, at < links)
        on = joined_ref[0, jnp.clip(at, 0, links - 1)] != 0
        return jnp.where(jnp.logical_and(inside, on), neighbour, ZERO).astype(jnp.int32)

    meta_ref[HELD] = held
    for i in range(SLOTS):
        left = joined_to(start + i - 1, EDGE if i == 0 else i - 1)
        right = joined_to(start + i, jnp.where(i >= last, EDGE, i + 1))
        meta_ref[L_IDX + i] = jnp.where(i < held, left, ZERO).astype(jnp.int32)
        meta_ref[R_IDX + i] = jnp.where(i < held, right, ZERO).astype(jnp.int32)
    meta_ref[L_IDX + EDGE] = joined_to(start + last, last)
    meta_ref[R_IDX + EDGE] = joined_to(start - 1, 0)

    for copy in firsts:
        copy.wait()
    even = me % 2 == 0

    def payload(slot, x_first, g_col):
        return (
            nt_dot(edge_select(2 * TH, x_lane(x_first)), xbuf[slot]).astype(BF),
            nt_dot(edge_select(TH, g_lane(g_col)), gbuf[slot]).astype(BF),
        )

    left_x, left_g = payload(0, 0, 0)
    for copy in loads:
        copy.wait()
    right_x, right_g = payload(last, TW - 2, TW - 1)

    @pl.when(even)
    def _():
        core_ref[: 2 * TH] = right_x
        core_ref[2 * TH :] = right_g
        other_ref[: 2 * TH] = left_x
        other_ref[2 * TH :] = left_g

    @pl.when(jnp.logical_not(even))
    def _():
        core_ref[: 2 * TH] = left_x
        core_ref[2 * TH :] = left_g
        other_ref[: 2 * TH] = right_x
        other_ref[2 * TH :] = right_g


def prep_kernel(
    x_ref, wr_ref, we_ref, wg_ref, s1_ref, b1_ref, s2_ref, b2_ref, s3_ref, b3_ref,
    hid_ref, slope_ref, dense_ref, denset_ref, wet_ref, mid_ref, end_ref, part_ref, win_ref,
):
    scale = column(s1_ref)
    shift = column(b1_ref)
    mid_ref[0] = scale
    mid_ref[1] = shift
    mid_ref[2] = column(s2_ref)
    mid_ref[3] = column(b2_ref)
    end_ref[0] = column(s3_ref)
    end_ref[1] = column(b3_ref)
    for half in range(SLOTS // 2):
        tiles = jnp.concatenate([x_ref[2 * half], x_ref[2 * half + 1]], axis=1)
        reduced = nn_dot(wr_ref[...], tiles)
        for k in range(2):
            i = 2 * half + k
            pre = reduced[:, k * PIX : (k + 1) * PIX] * scale + shift
            sig = sigmoid(pre)
            act = pre * sig
            hid_ref[i] = act.astype(BF)
            slope_ref[i] = (sig + act * (1.0 - sig)) * scale
    tap_row = lax.broadcasted_iota(jnp.int32, (TAPS * GW, KDIM), 0)
    lane = lax.broadcasted_iota(jnp.int32, (TAPS * GW, KDIM), 1)
    block = lane // HALF
    tap = 3 * (block % 3) + jnp.where(block < 3, 1, jnp.where(block < 6, 0, 2))
    pick = (tap_row == tap * GW + lane % GW).astype(F32).astype(BF)
    spread = tn_dot(wg_ref[...], pick)
    row = lax.broadcasted_iota(jnp.int32, (MID, KDIM), 0)
    col = lax.broadcasted_iota(jnp.int32, (MID, KDIM), 1)
    keep = (row % HALF) // GW == (col % HALF) // GW
    dense_ref[...] = jnp.where(keep, spread, 0.0).astype(BF).reshape(2, HALF, KDIM)
    row_t = lax.broadcasted_iota(jnp.int32, (HALF, MID), 0)
    col_t = lax.broadcasted_iota(jnp.int32, (HALF, MID), 1)
    keep_t = row_t // GW == (col_t % HALF) // GW
    prow = lax.broadcasted_iota(jnp.int32, (HALF, TAPS * GW), 0)
    pcol = lax.broadcasted_iota(jnp.int32, (HALF, TAPS * GW), 1)
    for k in range(TAPS):
        pick_t = (pcol == k * GW + prow % GW).astype(F32).astype(BF)
        spread_t = jnp.where(keep_t, nn_dot(pick_t, wg_ref[...]), 0.0).astype(BF)
        for b in range(2):
            denset_ref[b, :, k * HALF : (k + 1) * HALF] = spread_t[:, b * HALF : (b + 1) * HALF]
    wet_ref[...] = jnp.transpose(we_ref[...])
    lane = lax.broadcasted_iota(jnp.int32, (HALF, PIX), 1)
    for i in range(SLOTS):
        for b in range(2):
            shifts = row_shifts(hid_ref[i, b * HALF : (b + 1) * HALF, :], lane >= TW, lane < PIX - TW)
            for u, shifted in enumerate(shifts):
                win_ref[b, u * HALF : (u + 1) * HALF, i * PIX : (i + 1) * PIX] = shifted
    for b in range(2):
        part_ref[b * HALF : (b + 1) * HALF, :] = nn_dot(dense_ref[b, :, :MIDDLE], win_ref[b])


def silu_slope(v):
    sig = sigmoid(v)
    act = v * sig
    return act, sig + act * (1.0 - sig)


MIDDLE = 3 * HALF


def forward_place(u, v):
    return (1, 0, 2)[v] * 3 + u


def side_place(u, v):
    return None if v == 1 else forward_place(u, v) - 3


def transposed_place(u, v):
    return TAPS - 1 - (3 * u + v)


def row_shifts(base, has_above, has_below):
    zero = jnp.zeros((), BF)
    return (
        jnp.where(has_above, pltpu.roll(base, TW, 1), zero),
        base,
        jnp.where(has_below, pltpu.roll(base, PIX - TW, 1), zero),
    )


def build_windows(field_ref, win_ref, meta_ref, tiles, first, place):
    lane = lax.broadcasted_iota(jnp.int32, (HALF, PIX), 1)
    col = lane % TW
    first_col = col == 0
    last_col = col == TW - 1
    has_above = lane >= TW
    has_below = lane < PIX - TW
    for i in tiles:
        left_at = meta_ref[L_IDX + i]
        right_at = meta_ref[R_IDX + i]
        lanes = pl.ds((i - first) * PIX, PIX)
        for b in range(2):
            rows = pl.ds(b * HALF, HALF)
            own = field_ref[i, rows, :]
            left = field_ref[left_at, rows, :]
            right = field_ref[right_at, rows, :]
            west = jnp.where(first_col, pltpu.roll(left, PIX - TW + 1, 1), pltpu.roll(own, 1, 1))
            east = jnp.where(last_col, pltpu.roll(right, TW - 1, 1), pltpu.roll(own, PIX - 1, 1))
            for v, base in enumerate((west, own, east)):
                if place(0, v) is None:
                    continue
                for u, shifted in enumerate(row_shifts(base, has_above, has_below)):
                    win_ref[b, pl.ds(place(u, v) * HALF, HALF), lanes] = shifted


CHUNKS = ((0, 2), (2, 2))


def forward_kernel(
    devices, meta_ref, core_ref, other_ref, hid_in, wr_ref, dense_ref, wet_ref, mid_ref, end_ref, part_ref, x_ref, g_ref,
    out_ref, back_ref, errc_ref, slopeb_ref, hid_ref, edge_ref, hide_ref, slopee_ref, send_ref, keep_ref,
    win_ref, wine_ref, hidb_ref,
):
    me = lax.axis_index("tile")
    held = meta_ref[HELD]
    odd = me % 2
    core_first = jnp.where(odd == 0, 0, TW - 2)
    other_first = jnp.where(odd == 0, TW - 2, 0)
    edge_x = (
        tn_dot(core_ref[: 2 * TH, :], edge_select(2 * TH, x_lane(core_first)))
        + tn_dot(other_ref[: 2 * TH, :], edge_select(2 * TH, x_lane(other_first)))
    ).astype(BF)
    edge_ref[...] = edge_x
    for i in range(SLOTS):
        hid_ref[i] = hid_in[i]
    pre = nn_dot(wr_ref[...], edge_x) * mid_ref[0] + mid_ref[1]
    hid_ref[EDGE] = (pre * sigmoid(pre)).astype(BF)
    hid_ref[ZERO] = jnp.zeros((MID, PIX), BF)

    build_windows(hid_ref, wine_ref, meta_ref, (EDGE,), EDGE, forward_place)
    for b in range(2):
        rows = slice(b * HALF, (b + 1) * HALF)
        act, slope = silu_slope(nn_dot(dense_ref[b], wine_ref[b]) * mid_ref[2, rows, :] + mid_ref[3, rows, :])
        hide_ref[rows, :] = act.astype(BF)
        slopee_ref[rows, :] = slope * mid_ref[2, rows, :]

    for first, count in CHUNKS:
        build_windows(hid_ref, win_ref, meta_ref, range(first, first + count), 0, side_place)
        lanes = slice(first * PIX, (first + count) * PIX)
        for b in range(2):
            rows = slice(b * HALF, (b + 1) * HALF)
            conv = nn_dot(dense_ref[b, :, MIDDLE:], win_ref[b, :, lanes]) + part_ref[rows, lanes]
            for k in range(count):
                at = slice((first + k) * PIX, (first + k + 1) * PIX)
                act, slope = silu_slope(conv[:, k * PIX : (k + 1) * PIX] * mid_ref[2, rows, :] + mid_ref[3, rows, :])
                hidb_ref[rows, at] = act.astype(BF)
                slopeb_ref[rows, at] = slope * mid_ref[2, rows, :]
        grown = nn_dot(wet_ref[...], hidb_ref[:, lanes])
        for k in range(count):
            i = first + k
            act, slope = silu_slope(
                grown[:, k * PIX : (k + 1) * PIX] * end_ref[0] + end_ref[1] + x_ref[i].astype(F32)
            )
            live = jnp.where(i < held, 1.0, 0.0).astype(F32)
            back = g_ref[i].astype(F32) * slope * live
            out_ref[i] = (act * live).astype(BF)
            back_ref[i] = back
            errc_ref[:, i * PIX : (i + 1) * PIX] = (back * end_ref[0]).astype(BF)

    own = SLOTS * PIX
    for ref, flip in ((send_ref, 1), (keep_ref, 0)):
        rows = jnp.concatenate([hidb_ref[at, :own] for at in row_blocks(devices, me, flip)], axis=0)
        part = nt_dot(rows, errc_ref[:, :own]).astype(BF)
        per = MID // devices
        for j in range(devices // 2):
            for c in range(CIN // PIX):
                ref[j, c * per : (c + 1) * per, :] = part[j * per : (j + 1) * per, c * PIX : (c + 1) * PIX]


def row_blocks(devices, me, flip):
    per = MID // devices
    bits = (devices // 2).bit_length() - 1
    blocks = []
    for j in range(devices // 2):
        distance = flip
        for bit in range(bits):
            distance |= ((j >> (bits - 1 - bit)) & 1) << (bit + 1)
        at = pl.multiple_of((me ^ distance) * per, per)
        blocks.append(pl.ds(at, per))
    return blocks


def pull_kernel(
    core_ref, other_ref, hide_ref, slopee_ref, wet_ref, end_ref,
    edge_ref, we_ref, errc_ref, slopeb_ref, errb_ref,
):
    odd = lax.axis_index("tile") % 2
    core_g = jnp.where(odd == 0, 0, TW - 1)
    other_g = jnp.where(odd == 0, TW - 1, 0)
    edge_g = (
        tn_dot(core_ref[2 * TH :, :], edge_select(TH, g_lane(core_g)))
        + tn_dot(other_ref[2 * TH :, :], edge_select(TH, g_lane(other_g)))
    )
    for first, count in CHUNKS:
        lanes = slice(first * PIX, (first + count) * PIX)
        pulled = nn_dot(we_ref[...], errc_ref[:, lanes])
        errb = (pulled * slopeb_ref[:, lanes]).astype(BF)
        for k in range(count):
            errb_ref[first + k] = errb[:, k * PIX : (k + 1) * PIX]
    grown = nn_dot(wet_ref[...], hide_ref[...])
    _, slope = silu_slope(grown * end_ref[0] + end_ref[1] + edge_ref[...].astype(F32))
    errc = (edge_g * slope * end_ref[0]).astype(BF)
    errb_ref[EDGE] = (nn_dot(we_ref[...], errc) * slopee_ref[...]).astype(BF)
    errb_ref[ZERO] = jnp.zeros((MID, PIX), BF)


def backward_kernel(
    devices, meta_ref, errb_ref, hid_ref, slope_ref, denset_ref, x_ref, place_ref,
    erra_ref, *rest,
):
    send_refs, keep_refs = rest[:4], rest[4:8]
    win_ref, flat_ref, groups_ref, kept_ref = rest[8:]
    me = lax.axis_index("tile")
    held = meta_ref[HELD]
    for first, count in CHUNKS:
        build_windows(errb_ref, win_ref, meta_ref, range(first, first + count), 0, transposed_place)
        lanes = slice(first * PIX, (first + count) * PIX)
        for b in range(2):
            conv = nn_dot(denset_ref[b], win_ref[b, :, lanes])
            rows = slice(b * HALF, (b + 1) * HALF)
            for k in range(count):
                i = first + k
                live = jnp.where(i < held, 1.0, 0.0).astype(F32)
                err = (conv[:, k * PIX : (k + 1) * PIX] * slope_ref[i, rows, :] * live).astype(BF)
                flat_ref[rows, i * PIX : (i + 1) * PIX] = err
                erra_ref[i, rows, :] = err
    row = lax.broadcasted_iota(jnp.int32, (HALF, HALF), 0)
    col = lax.broadcasted_iota(jnp.int32, (HALF, HALF), 1)
    same = row // GW == col // GW
    for b in range(2):
        rows = slice(b * HALF, (b + 1) * HALF)
        hid = jnp.transpose(jnp.concatenate([hid_ref[i, rows, :] for i in range(SLOTS)], axis=1))
        for k in range(TAPS):
            full = nn_dot(win_ref[b, k * HALF : (k + 1) * HALF, :], hid)
            kept_ref[:, k * HALF : (k + 1) * HALF] = jnp.where(same, full, 0.0).astype(BF)
        groups_ref[rows, :] = nn_dot(kept_ref[...], place_ref[...]).astype(BF)
    tiles = jnp.concatenate([x_ref[i] for i in range(SLOTS)], axis=1)
    per = MID // devices
    inner = devices // 8
    lane = lax.broadcasted_iota(jnp.int32, (HALF, PIX), 1)
    row = lax.broadcasted_iota(jnp.int32, (HALF, PIX), 0)
    own_lanes = lane // GW == row % 8
    lane = lax.broadcasted_iota(jnp.int32, (PIX, PIX), 1)
    row = lax.broadcasted_iota(jnp.int32, (PIX, PIX), 0)
    repeat = (lane % GW == row).astype(F32).astype(BF)
    pack = lax.broadcasted_iota(jnp.int32, (4 * devices, HALF), 0)
    row = lax.broadcasted_iota(jnp.int32, (4 * devices, HALF), 1)
    gather = jnp.logical_and(pack // 8 == row // per, pack % 8 == (row % per) // 8).astype(F32).astype(BF)
    for refs, flip in ((send_refs, 1), (keep_refs, 0)):
        blocks = row_blocks(devices, me, flip)
        rows = jnp.concatenate([flat_ref[at, :] for at in blocks], axis=0)
        group_rows = jnp.concatenate([groups_ref[at, :] for at in blocks], axis=0)
        part = nt_dot(rows, tiles).astype(BF)
        tail = jnp.where(own_lanes, nn_dot(group_rows[:, PIX:], repeat), 0.0).astype(BF)
        tail = nn_dot(gather, tail).astype(BF)
        for j in range(devices // 2):
            ref, i = refs[j // inner], j % inner
            at = slice(j * per, (j + 1) * per)
            for c in range(CIN // PIX):
                ref[i, c * per : (c + 1) * per, :] = part[at, c * PIX : (c + 1) * PIX]
            ref[i, 8 * per : 9 * per, :] = group_rows[at, :PIX]
            ref[i, 9 * per :, :] = tail[8 * j : 8 * j + 8]


def grad_kernel(wr_ref, erra_ref, back_ref, act_ref, grad_ref, out_ref):
    out_ref[...] = act_ref[...]
    for half in range(SLOTS // 2):
        err = jnp.concatenate([erra_ref[2 * half], erra_ref[2 * half + 1]], axis=1)
        pulled = tn_dot(wr_ref[...], err)
        for k in range(2):
            i = 2 * half + k
            grad_ref[i] = (pulled[:, k * PIX : (k + 1) * PIX] + back_ref[i]).astype(BF)


def finish_kernel(norm, ea_ref, eb_ref, *refs):
    parts, (reduce_ref, group_ref, expand_ref) = refs[:4], refs[4:]
    expand = (ea_ref[...].astype(F32) + eb_ref[...].astype(F32)) * norm
    total = sum(part[...].astype(F32) for part in parts) * norm
    per = reduce_ref.shape[0]
    for c in range(CIN // PIX):
        reduce_ref[:, c * PIX : (c + 1) * PIX] = total[c * per : (c + 1) * per]
        expand_ref[:, c * PIX : (c + 1) * PIX] = expand[c * per : (c + 1) * per]
    group_ref[:, :PIX] = total[8 * per : 9 * per]
    tail = jnp.concatenate(
        [jnp.broadcast_to(total[9 * per + k : 9 * per + k + 1], (8, PIX)) for k in range(per // 8)], axis=0
    )
    lane = lax.broadcasted_iota(jnp.int32, (per, PIX), 1)
    row = lax.broadcasted_iota(jnp.int32, (per, PIX), 0)
    tail = jnp.where(lane // GW == row % 8, tail, 0.0)
    for shift in (64, 32, 16):
        tail = tail + pltpu.roll(tail, shift, 1)
    group_ref[:, PIX:] = tail[:, : TAPS * GW - PIX]


LIMITS = {"edges": 56, "prep": 18, "forward": 25, "pull": 12, "backward": 18, "grads": 9, "finish": 2}
WORK = {"edges": 2, "prep": 3, "forward": 7, "pull": 2, "backward": 5, "grads": 2, "finish": 1}


def call(body, name, out_shape, in_smem, in_any, n_in, scratch=(), out_smem=()):
    vmem = pl.BlockSpec(memory_space=pltpu.VMEM)
    smem = pl.BlockSpec(memory_space=pltpu.SMEM)
    anys = pl.BlockSpec(memory_space=pltpu.HBM)
    return pl.pallas_call(
        body,
        name=name,
        out_shape=out_shape,
        in_specs=[smem if i in in_smem else anys if i in in_any else vmem for i in range(n_in)],
        out_specs=[smem if i in out_smem else vmem for i in range(len(out_shape))],
        scratch_shapes=list(scratch),
        compiler_params=pltpu.CompilerParams(vmem_limit_bytes=LIMITS[name] * 1024 * 1024),
        cost_estimate=pl.CostEstimate(flops=int(WORK[name] * 1.1e9), bytes_accessed=1 << 20, transcendentals=0),
    )


def shape(dims, dtype):
    return jax.ShapeDtypeStruct(dims, dtype)


def swap(value, axis, mask):
    size = lax.axis_size(axis)
    return lax.ppermute(value, axis, [(i, i ^ mask) for i in range(size)])


def tap_places():
    row = np.arange(KDIM)
    place = np.zeros((KDIM, HALF), np.float32)
    place[row, row // HALF * GW + row % GW] = 1.0
    return jnp.asarray(place, BF)


def cross(value, devices, slides, tile_mask, slide_mask):
    pairs = [
        (t * slides + k, (t ^ tile_mask) * slides + (k ^ slide_mask))
        for t in range(devices)
        for k in range(slides)
    ]
    return lax.ppermute(value, ("tile", "slide"), pairs)


def spread(part, devices, slides):
    rows = part.shape[0] // 4
    return [part[:rows]] + [
        cross(part[k * rows : (k + 1) * rows], devices, slides, 2 * (k // 2 + 2 * (k % 2)), 0) for k in (1, 2, 3)
    ]


def add_all(first, *others):
    total = first.astype(F32)
    for other in others:
        total = total + other.astype(F32)
    return total.astype(BF)


def add_pair(a, b):
    return add_all(a, b)


def halve(part, mask):
    rows = part.shape[0] // 2
    return add_pair(part[:rows], swap(part[rows:], "tile", mask))


def shards(
    feats, cotangent, w_reduce, w_group, w_expand, scale1, shift1, scale2, shift2,
    scale3, shift3, tile_count, joined,
):
    devices = lax.axis_size("tile")
    slides = lax.axis_size("slide")
    per = MID // devices
    x, g = feats[0], cotangent[0]
    s1, b1, s2, b2 = (v.reshape(1, MID) for v in (scale1, shift1, scale2, shift2))
    s3, b3 = (v.reshape(1, CIN) for v in (scale3, shift3))

    to_core, to_other, meta = call(
        edge_kernel, "edges",
        [shape((PAY, CIN), BF), shape((PAY, CIN), BF), shape((META,), jnp.int32)],
        (), (0, 1, 2, 3), 4,
        [pltpu.SMEM(tile_count.shape, jnp.int32), pltpu.SMEM(joined.shape, jnp.int32),
         pltpu.VMEM((SLOTS, CIN, PIX), BF), pltpu.VMEM((SLOTS, CIN, PIX), BF), pltpu.SemaphoreType.DMA((6,))],
        (2,),
    )(tile_count, joined, x, g)
    hops = [(i, i + 1) for i in range(1, devices - 1, 2)]
    from_other = lax.ppermute(to_other, "tile", hops + [(b, a) for a, b in hops])
    from_core = swap(to_core, "tile", 1)

    hid, slope_a, dense, denset, wet, mid, end, part = call(
        prep_kernel, "prep",
        [shape((SLOTS, MID, PIX), BF), shape((SLOTS, MID, PIX), F32), shape((2, HALF, KDIM), BF),
         shape((2, HALF, KDIM), BF), shape((CIN, MID), BF), shape((4, MID, PIX), F32), shape((2, CIN, PIX), F32),
         shape((MID, SLOTS * PIX), F32)],
        (), (), 10, [pltpu.VMEM((2, MIDDLE, SLOTS * PIX), BF)],
    )(x, w_reduce, w_expand, w_group.T, s1, b1, s2, b2, s3, b3)

    lanes = SLOTS * PIX
    act, back, errc, slope_b, hid, edge, hid_e, slope_e, e_send, e_keep = call(
        functools.partial(forward_kernel, devices), "forward",
        [shape((SLOTS, CIN, PIX), BF), shape((SLOTS, CIN, PIX), F32), shape((CIN, lanes), BF),
         shape((MID, lanes), F32), shape((SLOTS + 2, MID, PIX), BF), shape((CIN, PIX), BF),
         shape((MID, PIX), BF), shape((MID, PIX), F32), shape((devices // 2, 8 * per, PIX), BF), shape((devices // 2, 8 * per, PIX), BF)],
        (0,), (), 12,
        [pltpu.VMEM((2, KDIM - MIDDLE, lanes), BF), pltpu.VMEM((2, KDIM, PIX), BF), pltpu.VMEM((MID, lanes), BF)],
    )(meta, from_core, from_other, hid, w_reduce, dense, wet, mid, end, part, x, g)

    e_core = swap(e_send, "tile", 1)
    (errb,) = call(
        pull_kernel, "pull", [shape((SLOTS + 2, MID, PIX), BF)], (), (), 10,
    )(from_core, from_other, hid_e, slope_e, wet, end, edge, w_expand, errc, slope_b)
    e_part = add_pair(e_keep, e_core)
    errb, e_part = lax.optimization_barrier((errb, e_part))
    e_part = halve(e_part, 2)

    piece = [shape((devices // 8, 9 * per + 8, PIX), BF)] * 8
    erra, *pieces = call(
        functools.partial(backward_kernel, devices), "backward", [shape((SLOTS, MID, PIX), BF)] + piece,
        (0,), (), 7,
        [pltpu.VMEM((2, KDIM, lanes), BF), pltpu.VMEM((MID, lanes), BF), pltpu.VMEM((MID, HALF), BF),
         pltpu.VMEM((HALF, KDIM), BF)],
    )(meta, errb, hid, slope_a, denset, x, tap_places())
    (grad_in, out) = call(
        grad_kernel, "grads", [shape((SLOTS, CIN, PIX), BF), shape((SLOTS, CIN, PIX), BF)], (), (), 4,
    )(w_reduce, erra, back, act)

    r_core = [swap(value, "tile", 1) for value in pieces[:4]]
    *r_core, e_part = lax.optimization_barrier((*r_core, e_part))
    r_parts = [add_pair(a, b) for a, b in zip(pieces[4:], r_core)]
    tall, half = r_parts[1].shape[1], e_part.shape[0] // 2
    r_parts[1] = jnp.concatenate([r_parts[1], e_part[half:]], axis=1)
    r_parts = [r_parts[0]] + [cross(r_parts[k], devices, slides, 2 * (k // 2 + 2 * (k % 2)), 0) for k in (1, 2, 3)]
    e_part = add_pair(e_part[:half], r_parts[1][:, tall:])
    r_parts[1] = r_parts[1][:, :tall]
    mask = 8
    while mask < devices:
        e_part = halve(e_part, mask)
        mask *= 2
    r_part = add_all(*r_parts)
    mask = 8
    while 2 * mask < devices:
        r_part = halve(r_part, mask)
        mask *= 2
    mine, theirs = r_part[0], r_part[1]
    near = mine.shape[0]
    both = cross(jnp.concatenate([mine, e_part[0]], axis=0), devices, slides, 0, 1)
    e_other = both[near:]
    finals = [
        mine,
        both[:near],
        cross(theirs, devices, slides, devices // 2, 0),
        cross(theirs, devices, slides, devices // 2, 1),
    ]
    if slides > 2:
        e_part, e_other = add_pair(e_part, e_other[None]), jnp.zeros_like(e_other)
        total = add_all(*finals)
        mask = 2
        while mask < slides:
            e_part = add_pair(e_part, swap(e_part, "slide", mask))
            total = add_pair(total, swap(total, "slide", mask))
            mask *= 2
        finals = [total] + [jnp.zeros_like(total)] * 3
    norm = 1.0 / math.sqrt(slides * LIVE_DEV * devices * PIX)
    grad_reduce, grad_group, grad_expand = call(
        functools.partial(finish_kernel, norm), "finish",
        [shape((per, CIN), F32), shape((per, TAPS * GW), F32), shape((per, CIN), F32)], (), (), 6,
    )(e_part[0], e_other, *finals)
    return (out[None], grad_in[None], grad_reduce, grad_group, grad_expand)


def solution(mesh):
    tiles = P("slide", "tile", None, None)
    in_specs = (tiles, tiles) + (P(),) * 9 + (P("slide", None), P("slide", None))
    out_specs = (tiles, tiles, P("tile", None), P("tile", None), P("tile", None))
    return jax.shard_map(shards, mesh=mesh, in_specs=in_specs, out_specs=out_specs, check_vma=False)
```
